32 devices in a mesh: groups: 2 (over x), example: 8 (over z, y), cls: 2 (over core).
Axes of the slice: x: 2, y: 2, z: 4, core: 2. Of those that a mesh axis runs over, the one named last changes fastest.
Arguments:
- features: bfloat16 [2048, 4096], P(('groups', 'example'), 'cls'), parts along dimension 0
- weights: float32 [8192, 8192], P(('groups', 'cls'), 'example'), parts along dimension 0
- labels: int32 [2048], P(('groups', 'example')), parts along dimension 0, may hold values from 0 to 8191
- counts: int32 [16], P(('groups', 'example')), parts along dimension 0, may hold values from 16 to 128, as said below
- active: int32 [2], P('groups'), parts along dimension 0, may hold values from 4096 to 8192
Outputs:
- moved: float32 [8192, 8192], P(('groups', 'cls'), 'example'), parts along dimension 0
- losses: float32 [2048], P(('groups', 'example')), parts along dimension 0
The draws below stay inside these ranges and needn't reach their ends.
There are 2 independent parts, one for each index of `groups`. The reference program is written for one: setup_inputs(seed, part) draws one part's arguments, and reference() takes and returns one part's arrays. A program takes and returns all parts, laid end to end along the dimension named above; each array names one. Nothing has to cross between parts.
Inputs may be any that keep to these rules, and one draw needn't show every extreme that they name: `counts`: each block has at least 16 valid slots; some block is full in every draw.
All inputs are finite; a program needn't handle non-finite values.
Results may differ from the reference program's by a relative error of at most 0.006.
Values may be sent and summed in bfloat16 or wider, within the bound.
A program may use at most 128 MiB of HBM per device.

```python
import math
import jax
import jax.numpy as jnp
import numpy as np

FEATURES = 4096
CLASSES = 8192
EX_DEV = 128
ITERS = 2
EXAMPLES = 1024


def draw_features(key, part):
    feature_pos = jnp.arange(FEATURES).astype(jnp.float32) / FEATURES
    rough = jnp.exp(jax.random.uniform(jax.random.fold_in(key, 1), (FEATURES,), jnp.float32, jnp.log(0.7), jnp.log(1.4)))
    col_scale = 0.4 * jnp.power(10.0, feature_pos) * rough
    row_scale = jnp.exp(jax.random.uniform(jax.random.fold_in(key, 2), (EXAMPLES, 1), jnp.float32, jnp.log(0.6), jnp.log(1.6)))
    base = jax.random.truncated_normal(jax.random.fold_in(key, 3), -4.0, 4.0, (EXAMPLES, FEATURES), jnp.float32)
    values = base * row_scale * col_scale
    return values.astype(jnp.bfloat16)


def draw_weights(key, part):
    class_scale = jnp.exp(jax.random.uniform(jax.random.fold_in(key, 21), (1, CLASSES), jnp.float32, jnp.log(0.5), jnp.log(5.0)))
    base = jax.random.truncated_normal(jax.random.fold_in(key, 22), -4.0, 4.0, (FEATURES, CLASSES), jnp.float32)
    values = base * class_scale / jnp.sqrt(float(FEATURES))
    return values


def draw_counts(key, part):
    blocks = EXAMPLES // EX_DEV
    lowest = max(EX_DEV // 8, 1)
    first_draw = jax.random.randint(jax.random.fold_in(key, 31), (blocks,), lowest, EX_DEV + 1)
    second_draw = jax.random.randint(jax.random.fold_in(key, 32), (blocks,), lowest, EX_DEV + 1)
    full_block = jax.random.randint(jax.random.fold_in(key, 33), (), 0, blocks)
    values = jnp.minimum(first_draw, second_draw)
    return jnp.where(jnp.arange(blocks) == full_block, EX_DEV, values).astype(jnp.int32)


def plant(drawn, rng, low, top_value):
    longest = drawn.shape.index(max(drawn.shape))
    spots = []
    for shift in (0, 1):
        where = [jax.random.randint(jax.random.fold_in(rng, axis), (), 0, length) for axis, length in enumerate(drawn.shape)]
        where[longest] = (where[longest] + shift) % drawn.shape[longest]
        spots.append(tuple(where))
    return drawn.at[spots[0]].set(low).at[spots[1]].set(top_value)


def cumulative_ranks(amount, skew):
    weights = [(1 << 20) // math.isqrt(rank ** skew) + 1 for rank in range(1, amount + 1)]
    spread = 1 + sum(weights) // (1 << 30)
    return np.cumsum(np.array([max(1, weight // spread) for weight in weights]))


def skewed_ids(own_key, dims, amount, slope):
    grid = cumulative_ranks(amount, slope)
    lot = jax.random.randint(jax.random.fold_in(own_key, 1), dims, 0, int(grid[amount - 1]))
    grade = jnp.searchsorted(jnp.asarray(grid, jnp.int32), lot, side="right")
    return jax.random.permutation(jax.random.fold_in(own_key, 2), amount)[grade].astype(jnp.int32)


def setup_inputs(seed: int = 0, part: int = 0) -> dict:
    arg_keys = jax.random.split(jax.random.key(seed), 6)
    part_keys = jax.random.split(jax.random.fold_in(arg_keys[5], part), 6)
    features = draw_features(jax.random.fold_in(jax.random.fold_in(arg_keys[5], part), 71), part)
    weights = draw_weights(jax.random.fold_in(jax.random.fold_in(arg_keys[5], part), 71), part)
    labels = plant(skewed_ids(part_keys[2], (EXAMPLES,), CLASSES, 2), jax.random.fold_in(part_keys[2], 3), 0, CLASSES - 1).astype(jnp.int32)
    counts = draw_counts(jax.random.fold_in(jax.random.fold_in(arg_keys[5], part), 71), part)
    active = jax.random.randint(part_keys[4], (1,), CLASSES // 2, CLASSES + 1).astype(jnp.int32)
    return {"features": features, "weights": weights, "labels": labels, "counts": counts, "active": active}


NEGATIVE = -1e30
LEARNING_RATE = 2e-5
DAMPING_SHARE = 0.1
EPSILON = 1e-6


def reference(features, weights, labels, counts, active):
    row_index = jnp.arange(EXAMPLES)
    is_valid = ((row_index % EX_DEV) < counts[row_index // EX_DEV]).astype(jnp.float32)
    valid_total = jnp.sum(counts).astype(jnp.float32)
    active_count = active[0]
    target = (labels % active_count).astype(jnp.int32)
    class_index = jnp.arange(CLASSES)
    is_active = class_index < active_count
    is_label = class_index[None, :] == target[:, None]
    squares = (features.astype(jnp.float32) * features.astype(jnp.float32)).astype(jnp.bfloat16)
    current = weights
    moved = jnp.zeros_like(weights)
    denominator = None
    losses = None
    for iteration in range(ITERS):
        current_low = current.astype(jnp.bfloat16)
        logits = jnp.dot(features, current_low, preferred_element_type=jnp.float32)
        masked = jnp.where(is_active[None, :], logits, NEGATIVE)
        row_peak = jnp.max(masked, axis=1)
        exponent = jnp.exp(masked - row_peak[:, None])
        row_total = jnp.sum(exponent, axis=1)
        label_logit = jnp.sum(jnp.where(is_label, logits, 0.0), axis=1)
        probability = exponent / row_total[:, None]
        residual = (is_valid[:, None] * (probability - is_label.astype(jnp.float32)) / valid_total).astype(jnp.bfloat16)
        gradient = jnp.dot(features.T, residual, preferred_element_type=jnp.float32)
        if iteration == 0:
            fisher_weight = (is_valid[:, None] * probability * (1.0 - probability) / valid_total).astype(jnp.bfloat16)
            fisher = jnp.dot(squares.T, fisher_weight, preferred_element_type=jnp.float32)
            damping = DAMPING_SHARE * jnp.sum(fisher) / (FEATURES * CLASSES) + EPSILON
            denominator = fisher + damping
        change = gradient / denominator
        current = current - LEARNING_RATE * change
        moved = moved - change
        losses = is_valid * (row_peak + jnp.log(row_total) - label_logit)
    return moved, losses
```

```python
import functools

import jax
import jax.numpy as jnp
from jax import lax
from jax.experimental import pallas as pl
from jax.experimental.pallas import tpu as pltpu
from jax.sharding import PartitionSpec as P

ITERS = 2
NEGATIVE = -1e30
LEARNING_RATE = 2e-05
DAMPING_SHARE = 0.1
EPSILON = 1e-06
MESH = pl.DeviceIdType.MESH
UP, DOWN, SIDE, SIBLING = 0, 1, 2, 3
F32, BF16 = jnp.float32, jnp.bfloat16


def kernel(
    Z, Y, scale,
    features, weights, meta, active,
    moved, losses,
    x, xt, w, wlow, e_scr, r_scr, fw_scr, rec, g_scr,
    meta_all, stat1, stat2, damp_all, b_scr, ssq, loss_scr,
    own_sem, w_sem, gsend, grecv, wsend, wrecv, msend, mrecv,
    ssend, srecv, dsend, drecv, out_sem, osend, orecv,
):
    n = Z * Y
    nd = 2 * n
    rows_n = features.shape[0]
    half = features.shape[1]
    all_rows = n * rows_n
    ck = w.shape[2]
    me = lax.axis_index("example")
    k = lax.axis_index("cls")
    sib = 1 - k
    z, y = me // Y, lax.rem(me, Y)
    is_end = jnp.logical_or(z == 0, z == Z - 1)
    mine = me * 2 + k

    def rows(slot):
        return pl.ds(pl.multiple_of(slot * rows_n, rows_n), rows_n)

    def columns(index):
        return pl.ds(pl.multiple_of(index * ck, ck), ck)

    def remote(src, dst, ssem, rsem, example, core):
        return pltpu.make_async_remote_copy(
            src_ref=src, dst_ref=dst, send_sem=ssem, recv_sem=rsem,
            device_id={"example": example, "cls": core}, device_id_type=MESH,
        )

    own_copy = pltpu.make_async_copy(features, x.at[k, rows(me)], own_sem)
    own_copy.start()
    w_copy = pltpu.make_async_copy(weights.at[:, columns(k)], w.at[k], w_sem)
    w_copy.start()

    barrier = pltpu.get_barrier_semaphore()

    def greet(example, core):
        pl.semaphore_signal(
            barrier, inc=1, device_id={"example": example, "cls": core}, device_id_type=MESH
        )

    greet(me, sib)
    if Y == 2:
        greet(z * Y + (1 - y), k)

    @pl.when(z < Z - 1)
    def _():
        greet(me + Y, k)

    @pl.when(z > 0)
    def _():
        greet(me - Y, k)

    pl.semaphore_wait(barrier, Y + (z < Z - 1).astype(jnp.int32) + (z > 0).astype(jnp.int32))

    def forward(slot, direction, src, second=None):
        place = rows(slot)
        if second is not None:
            size = rows_n // 2
            place = pl.ds(pl.multiple_of(slot * rows_n + second * size, size), size)
            src = x.at[k, place]
        target, core = {
            UP: (me + Y, k),
            DOWN: (me - Y, k),
            SIDE: (z * Y + (Y - 1 - y), k),
            SIBLING: (me, sib),
        }[direction]
        return remote(
            src, x.at[k, place], gsend.at[direction, slot], grecv.at[k, slot], target, core
        )

    def landed(h, slot):
        remote(
            x.at[h, rows(slot)], x.at[h, rows(slot)], gsend.at[SIBLING, slot],
            grecv.at[h, slot], me, sib,
        ).wait_recv()

    meta_all[me] = meta[...]

    def meta_copy(p):
        peer = lax.rem(me + p, n)
        return peer, remote(
            meta, meta_all.at[me], msend.at[p], mrecv.at[me], peer, k
        )

    def meta_start(p, c):
        meta_copy(p)[1].start()
        return c

    def line(j, act, own=False):
        for sign in (1,) if own else (-1, 1):
            zz = z + sign * j
            slot = zz * Y + y
            src = features if own else x.at[k, rows(slot)]
            inside = jnp.logical_and(zz >= 0, zz < Z)

            @pl.when(inside)
            def _():
                act("enter", slot, None)
                if own or sign == -1:
                    @pl.when(z < Z - 1)
                    def _():
                        act("send", slot, forward(slot, UP, src))
                if own or sign == 1:
                    @pl.when(z > 0)
                    def _():
                        act("send", slot, forward(slot, DOWN, src))
                if Y == 2 and own:
                    act("send", slot, forward(slot, SIDE, src))
                elif Y == 2:
                    far = jnp.logical_and(is_end, j == Z - 1)
                    edge = jnp.logical_or(zz == 0, zz == Z - 1)
                    near = jnp.logical_and(jnp.logical_not(is_end), edge)
                    near = jnp.logical_and(near, j == 1)

                    @pl.when(far)
                    def _():
                        act("send", slot, forward(slot, SIDE, src, 0))

                    @pl.when(jnp.logical_not(jnp.logical_or(far, near)))
                    def _():
                        act("send", slot, forward(slot, SIDE, src))
                act("send", slot, forward(slot, SIBLING, src))

    def cross(j, slot, act):
        src = x.at[k, rows(slot)]

        @pl.when(jnp.logical_and(z == 0, j == 0))
        def _():
            act(forward(slot, UP, src))

        @pl.when(jnp.logical_and(z == Z - 1, j == 0))
        def _():
            act(forward(slot, DOWN, src))

        @pl.when(jnp.logical_and(z == 1, j == 2))
        def _():
            act(forward(slot, DOWN, src, 1))

        @pl.when(jnp.logical_and(z == 2, j == 2))
        def _():
            act(forward(slot, UP, src, 1))

        act(forward(slot, SIBLING, src))

    def begin(kind, slot, copy):
        if kind == "enter":
            landed(k, slot)
        else:
            copy.start()

    def begin_own(kind, slot, copy):
        if kind == "send":
            copy.start()

    def finish(kind, slot, copy):
        if kind == "send":
            copy.wait_send()

    line(0, begin_own, own=True)
    w_send = remote(weights.at[:, columns(sib)], w.at[k], wsend, wrecv, me, sib)
    w_send.start()

    def lower(h):
        step = min(512, half)

        def go(i, c):
            part = pl.ds(pl.multiple_of(i * step, step), step)
            wlow[h, part, :] = w[h, part, :].astype(BF16)
            return c

        lax.fori_loop(0, half // step, go, 0)

    w_copy.wait()
    lower(k)
    own_copy.wait()
    remote(w.at[sib], w.at[sib], wsend, wrecv, me, sib).wait_recv()
    lower(sib)

    def meta_wait(p, c):
        src = lax.rem(me + p, n)
        remote(meta, meta_all.at[src], msend.at[p], mrecv.at[src], me, sib).wait_recv()
        return c


    active_count = active[0]
    class_base = mine * ck
    class_index = class_base + lax.broadcasted_iota(jnp.int32, (rows_n, ck), 1)
    class_float = class_index.astype(F32)
    is_active = class_index < active_count
    lane = lax.broadcasted_iota(jnp.int32, (rows_n, rows_n), 1)

    def column(row):
        return jnp.broadcast_to(row, (rows_n, rows_n)).T[:, 0:1]

    def statistics(slot, logits, stat, with_label):
        masked = jnp.where(is_active, logits, NEGATIVE)
        peak = jnp.max(masked, axis=1, keepdims=True)
        exponent = jnp.exp(masked - peak)
        total = jnp.sum(exponent, axis=1, keepdims=True)
        e_scr[rows(slot), :] = exponent
        tile = jnp.where(lane == 0, peak, total)
        if with_label:
            target = column(meta_all[slot, 0:1, :])
            label = jnp.sum(
                jnp.where(class_float == target, logits, 0.0), axis=1, keepdims=True
            )
            tile = jnp.where(lane == 2, label, tile)
        tile = tile.T
        stat[mine, 0, pl.ds(slot, 1), :] = tile[0:1, :]
        stat[mine, 1, pl.ds(slot, 1), :] = tile[1:2, :]
        if with_label:
            stat[mine, 2, pl.ds(slot, 1), :] = tile[2:3, :]

    def process(slot):
        logits = None
        squares = None
        for h in range(2):
            block = x[h, rows(slot), :]
            xt[h, :, rows(slot)] = block.T
            term = jnp.sum((block * block).astype(F32), axis=1, keepdims=True)
            part = jnp.dot(block, wlow[h], preferred_element_type=F32)
            squares = term if h == 0 else squares + term
            logits = part if h == 0 else logits + part
        ssq[rows(slot), :] = jnp.broadcast_to(squares, (rows_n, 128))
        statistics(slot, logits, stat1, False)

    quarters = 2 * Y

    def gather(t, c):
        j, q = t // quarters, lax.rem(t, quarters)

        @pl.when(q == quarters - 2)
        def _():
            line(j + 1, begin)

        zz = z + (2 * lax.rem(q, 2) - 1) * j
        yy = y if Y == 1 else jnp.where(q < 2, y, 1 - y)
        slot = zz * Y + yy
        inside = jnp.logical_and(zz >= 0, zz < Z)
        inside = jnp.logical_and(inside, jnp.logical_or(j > 0, lax.rem(q, 2) == 1))

        @pl.when(inside)
        def _():
            if Y == 2:
                @pl.when(q >= 2)
                def _():
                    landed(k, slot)
                    cross(j, slot, lambda copy: copy.start())

            landed(sib, slot)
            process(slot)

        return c

    lax.fori_loop(0, Z * quarters, gather, 0)

    def share(buffer, count, ssem, rsem):
        def piece(slot):
            return buffer.at[slot] if count is None else buffer.at[slot, pl.ds(0, count)]

        def copy(p):
            peer = lax.rem(mine + p, nd)
            return remote(
                piece(mine), piece(mine), ssem.at[p], rsem.at[mine], peer // 2, lax.rem(peer, 2)
            )

        def start(p, c):
            copy(p).start()
            return c

        def wait_in(p, c):
            src = lax.rem(mine + p, nd)
            remote(
                piece(src), piece(src), ssem.at[p], rsem.at[src], me, sib
            ).wait_recv()
            return c

        def wait_out(p, c):
            copy(p).wait_send()
            return c

        return (
            lambda: lax.fori_loop(1, nd, start, 0),
            lambda: lax.fori_loop(1, nd, wait_in, 0),
            lambda: lax.fori_loop(1, nd, wait_out, 0),
        )

    start1, in1, out1 = share(stat1, None, ssend.at[0], srecv.at[0])
    start1()
    lax.fori_loop(1, n, meta_start, 0)
    lax.fori_loop(1, n, meta_wait, 0)
    counts = meta_all[:, 1, :]
    valid_total = jnp.sum(counts[:, 0:1], axis=0, keepdims=True)

    def combine(stat):
        peak = stat[0, 0]
        for d in range(1, nd):
            peak = jnp.maximum(peak, stat[d, 0])
        total = jnp.zeros_like(peak)
        for d in range(nd):
            total = total + stat[d, 1] * jnp.exp(stat[d, 0] - peak)
        b_scr[...] = jnp.exp(stat[mine, 0] - peak) / total
        return peak, total

    row_number = lax.broadcasted_iota(jnp.int32, (rows_n, 1), 0).astype(F32)

    def residuals(first):
        def go(i, acc):
            valid = (row_number < meta_all[i, 1:2, 0:1]).astype(F32) / valid_total
            target = column(meta_all[i, 0:1, :])
            probability = e_scr[rows(i), :] * column(b_scr[pl.ds(i, 1), :])
            is_label = (class_float == target).astype(F32)
            r_scr[rows(i), :] = (valid * (probability - is_label)).astype(BF16)
            if first:
                fw = (valid * probability * (1.0 - probability)).astype(BF16)
                fw_scr[rows(i), :] = fw
                row_sum = jnp.sum(fw.astype(F32), axis=1, keepdims=True)
                acc = acc + jnp.sum(row_sum * ssq[rows(i), 0:1], axis=0, keepdims=True)
            return acc

        return lax.fori_loop(0, n, go, jnp.zeros((1, 1), F32), unroll=4)

    in1()
    combine(stat1)
    fisher_part = residuals(True)
    damp_all[mine] = jnp.broadcast_to(fisher_part, damp_all.shape[1:])
    start_d, in_d, out_d = share(damp_all, None, dsend, drecv)
    start_d()

    step = min(512, half)
    per_half = half // step

    def chunk(i):
        return i // per_half, pl.ds(pl.multiple_of(lax.rem(i, per_half) * step, step), step)

    def gradient(i, c):
        h, part = chunk(i)
        g_scr[h, part, :] = jnp.dot(xt[h, part, :], r_scr[...], preferred_element_type=F32)
        return c

    lax.fori_loop(0, 2 * per_half, gradient, 0, unroll=2)

    in_d()
    fisher_sum = damp_all[0, 0:1, 0:1]
    for d in range(1, nd):
        fisher_sum = fisher_sum + damp_all[d, 0:1, 0:1]
    damping = DAMPING_SHARE * fisher_sum / scale + EPSILON
    e_scr[...] = jnp.zeros_like(e_scr)

    big = min(1024, half)
    parts = half // big

    def fisher_step(i, c):
        h = i // parts
        part = pl.ds(pl.multiple_of(lax.rem(i, parts) * big, big), big)
        block = xt[h, part, :]
        fisher = jnp.dot(block * block, fw_scr[...], preferred_element_type=F32)
        inverse = 1.0 / (fisher + damping)
        rec[h, part, :] = inverse
        change = g_scr[h, part, :] * inverse
        g_scr[h, part, :] = change
        low = (w[h, part, :] - LEARNING_RATE * change).astype(BF16)
        wlow[h, part, :] = low
        e_scr[...] += jnp.dot(x[h, :, part], low, preferred_element_type=F32)
        return c

    lax.fori_loop(0, 2 * parts, fisher_step, 0)

    def second(i, c):
        statistics(i, e_scr[rows(i), :], stat2, True)
        return c

    lax.fori_loop(0, n, second, 0, unroll=4)
    start2, in2, out2 = share(stat2, None, ssend.at[1], srecv.at[1])
    start2()
    in2()
    peak, total = combine(stat2)
    label = stat2[0, 2]
    for d in range(1, nd):
        label = label + stat2[d, 2]
    lane_row = lax.broadcasted_iota(jnp.int32, (n, rows_n), 1).astype(F32)
    loss_scr[...] = (lane_row < counts).astype(F32) * (peak + jnp.log(total) - label)
    losses[...] = loss_scr[pl.ds(me, 1), :]
    residuals(False)

    def place(i):
        h = jnp.where(i < per_half, sib, k)
        return h, pl.ds(pl.multiple_of(lax.rem(i, per_half) * step, step), step)

    def out_remote(i):
        h, part = place(i)
        return remote(
            w.at[h, part, :], moved.at[part, columns(k)], osend.at[i], orecv.at[i], me, sib
        )

    def out_local(i):
        h, part = place(i)
        return pltpu.make_async_copy(
            w.at[h, part, :], moved.at[part, columns(k)], out_sem.at[i - per_half]
        )

    def last(i, c):
        h, part = place(i)
        grad = jnp.dot(xt[h, part, :], r_scr[...], preferred_element_type=F32)
        w[h, part, :] = -g_scr[h, part, :] - grad * rec[h, part, :]

        @pl.when(i < per_half)
        def _():
            out_remote(i).start()

        @pl.when(i >= per_half)
        def _():
            out_local(i).start()

        return c

    w_send.wait_send()
    lax.fori_loop(0, 2 * per_half, last, 0)

    line(0, finish, own=True)

    def drain(j, c):
        line(j, finish)
        return c

    lax.fori_loop(1, Z, drain, 0)
    if Y == 2:
        def drain_side(zz, c):
            slot = zz * Y + (1 - y)
            cross(jnp.abs(zz - z), slot, lambda copy: copy.wait_send())
            return c

        lax.fori_loop(0, Z, drain_side, 0)

    def meta_done(p, c):
        meta_copy(p)[1].wait_send()
        return c

    lax.fori_loop(1, n, meta_done, 0)
    out1()
    out_d()
    out2()

    def out_done(i, c):
        out_remote(i).wait_send()
        _, part = place(i)
        remote(
            w.at[k, part, :], moved.at[part, columns(sib)], osend.at[i], orecv.at[i], me, sib
        ).wait_recv()
        out_local(i + per_half).wait()
        return c

    lax.fori_loop(0, per_half, out_done, 0)


def solution(mesh):
    n = mesh.shape["example"]
    Y = 2 if n == 8 else 1
    Z = n // Y
    nd = 2 * n

    def body(features, weights, labels, counts, active):
        rows_n, half = features.shape
        local = weights.shape[1]
        ck = local // 2
        all_rows = rows_n * n
        target = (labels % active[0]).astype(F32)
        meta = jnp.concatenate(
            [
                target[None, :],
                jnp.broadcast_to(counts.astype(F32)[:, None], (7, rows_n)),
            ],
            axis=0,
        )
        scale = float(half * 2 * local * n)
        per_half = half // min(512, half)
        dma = pltpu.SemaphoreType.DMA
        moved, losses = pl.pallas_call(
            functools.partial(kernel, Z, Y, scale),
            out_shape=(
                pltpu.VMEM(weights.shape, F32),
                jax.ShapeDtypeStruct((1, rows_n), F32),
            ),
            in_specs=[
                pl.BlockSpec(memory_space=pl.ANY),
                pl.BlockSpec(memory_space=pl.ANY),
                pl.BlockSpec(memory_space=pltpu.VMEM),
                pl.BlockSpec(memory_space=pltpu.SMEM),
            ],
            out_specs=(
                pl.BlockSpec(memory_space=pltpu.VMEM),
                pl.BlockSpec(memory_space=pltpu.VMEM),
            ),
            scratch_shapes=[
                pltpu.VMEM((2, all_rows, half), BF16),
                pltpu.VMEM((2, half, all_rows), BF16),
                pltpu.VMEM((2, half, ck), F32),
                pltpu.VMEM((2, half, ck), BF16),
                pltpu.VMEM((all_rows, ck), F32),
                pltpu.VMEM((all_rows, ck), BF16),
                pltpu.VMEM((all_rows, ck), BF16),
                pltpu.VMEM((2, half, ck), F32),
                pltpu.VMEM((2, half, ck), F32),
                pltpu.VMEM((n, 8, rows_n), F32),
                pltpu.VMEM((nd, 2, n, rows_n), F32),
                pltpu.VMEM((nd, 3, n, rows_n), F32),
                pltpu.VMEM((nd, 8, 128), F32),
                pltpu.VMEM((n, rows_n), F32),
                pltpu.VMEM((all_rows, 128), F32),
                pltpu.VMEM((n, rows_n), F32),
                dma, dma,
                dma((4, n)), dma((2, n)),
                dma, dma,
                dma((n,)), dma((n,)),
                dma((2, nd)), dma((2, nd)),
                dma((nd,)), dma((nd,)),
                dma((per_half,)), dma((per_half,)), dma((per_half,)),
            ],
            compiler_params=pltpu.CompilerParams(
                collective_id=0, has_side_effects=True, vmem_limit_bytes=57671680
            ),
        )(features, weights, meta, active)
        return moved, losses.reshape(rows_n)

    return jax.shard_map(
        body,
        mesh=mesh,
        in_specs=(
            P(("groups", "example"), "cls"),
            P(("groups", "cls"), "example"),
            P(("groups", "example")),
            P(("groups", "example")),
            P("groups"),
        ),
        out_specs=(P(("groups", "cls"), "example"), P(("groups", "example"))),
        check_vma=False,
    )
```

```python
import functools

import jax
import jax.numpy as jnp
from jax import lax
from jax.experimental import pallas as pl
from jax.experimental.pallas import tpu as pltpu
from jax.sharding import PartitionSpec as P

NEGATIVE = -1e30
LEARNING_RATE = 2e-05
DAMPING_SHARE = 0.1
EPSILON = 1e-06
MESH = pl.DeviceIdType.MESH
INWARD, OUTWARD, SIDE = 0, 1, 2
F32, BF16 = jnp.float32, jnp.bfloat16

ROUNDS = 4
LANES = 128
HALF_ROWS = 512
AHEAD = 1
OWN_AT = 0
AT_END = "DCABEFG"
AT_END_LAG = (0, 1, 0, 0, 1, 1, 1)
AT_MID = "BFADGCE"
AT_MID_LAG = (0, 1, 0, 0, 1, 0, 1)
END_OFFSET = dict(A=1, B=2, C=3, D=0, E=1, F=2, G=3)
MID_OFFSET = dict(A=-1, B=1, C=2, D=0, E=1, F=-1, G=2)
TASK_L, TASK_R, TASK_OWN, TASK_SIB = 1, 2, 4, 6


def kernel(
    Z, Y, scale,
    features, weights, meta, active,
    moved, losses,
    x, xt, w, wlow, low_out, e_scr, r_scr, fw_scr, inv,
    meta_all, target_col, valid_col, ssq, fsum, stat1, stat2, damp_all, loss_col,
    own_sem, w_sem, gsend, grecv, sib_send, sib_recv,
    wsend, wrecv, lsend, lrecv, msend, mrecv,
    s1send, s1recv, s2send, s2recv, dsend, drecv,
    rsend, rrecv, fsend, frecv, r2send, r2recv,
):
    n = Z * Y
    nd = 2 * n
    rows_n, half = features.shape
    S = ROUNDS
    q = rows_n // S
    per_round = n * q
    groups = per_round // LANES
    all_rows = n * rows_n
    ck = moved.shape[1] // 2
    step = min(512, half)
    parts = half // step
    halves = all_rows // HALF_ROWS
    per_half = HALF_ROWS // LANES
    me = lax.axis_index("example")
    k = lax.axis_index("cls")
    sib = 1 - k
    z, y = me // Y, lax.rem(me, Y)
    mine = me * 2 + k
    inward = jnp.where(z < Z // 2, 1, -1)
    is_end = jnp.logical_or(z == 0, z == Z - 1)
    is_mid = jnp.logical_not(is_end)

    def round_rows(s):
        return pl.ds(pl.multiple_of(s * per_round, per_round), per_round)

    def piece_rows(s, slot):
        return pl.ds(pl.multiple_of(s * per_round + slot * q, q), q)

    def columns(c):
        return pl.ds(pl.multiple_of(c * ck, ck), ck)

    def feature_part(i):
        return pl.ds(pl.multiple_of(i * step, step), step)

    def remote(src, dst, ssem, rsem, example, core):
        return pltpu.make_async_remote_copy(
            src_ref=src, dst_ref=dst, send_sem=ssem, recv_sem=rsem,
            device_id={"example": example, "cls": core}, device_id_type=MESH,
        )

    def own_piece(s):
        return features.at[pl.ds(pl.multiple_of(s * q, q), q)]

    def own_copy(s):
        return pltpu.make_async_copy(own_piece(s), x.at[k, piece_rows(s, me)], own_sem.at[s])

    def w_copy(i):
        return pltpu.make_async_copy(
            weights.at[feature_part(i)], w.at[feature_part(i)], w_sem.at[i]
        )

    for s in range(S):
        own_copy(s).start()
    for i in range(parts):
        w_copy(i).start()

    barrier = pltpu.get_barrier_semaphore()

    def greet(example, core):
        pl.semaphore_signal(
            barrier, inc=1, device_id={"example": example, "cls": core}, device_id_type=MESH
        )

    greet(me, sib)
    if Y == 2:
        greet(z * Y + (1 - y), k)

    @pl.when(z < Z - 1)
    def _():
        greet(me + Y, k)

    @pl.when(z > 0)
    def _():
        greet(me - Y, k)

    pl.semaphore_wait(barrier, Y + (z < Z - 1).astype(jnp.int32) + (z > 0).astype(jnp.int32))

    def forward(direction, s, slot, src):
        target = {
            INWARD: me + inward * Y,
            OUTWARD: me - inward * Y,
            SIDE: z * Y + (Y - 1 - y),
        }[direction]
        return remote(
            src, x.at[k, piece_rows(s, slot)], gsend.at[direction, s, slot],
            grecv.at[s, slot], target, k,
        )

    def to_sibling(s, slot, src):
        return remote(
            src, x.at[k, piece_rows(s, slot)], sib_send.at[s], sib_recv.at[s], me, sib
        )

    def arrived(s, slot):
        place = x.at[k, piece_rows(s, slot)]
        remote(place, place, gsend.at[SIDE, s, slot], grecv.at[s, slot], me, sib).wait_recv()

    def has_outer():
        return jnp.logical_and(z - inward >= 0, z - inward < Z)

    def own_sends(s, act):
        src = own_piece(s)
        act(forward(INWARD, s, me, src))

        @pl.when(has_outer())
        def _():
            act(forward(OUTWARD, s, me, src))

        if Y == 2:
            act(forward(SIDE, s, me, src))

    def begin(copy):
        copy.start()

    def finish(copy):
        copy.wait_send()

    def event(p, i, receive, act):
        end, mid = AT_END[i], AT_MID[i]
        s = p - jnp.where(is_end, AT_END_LAG[i], AT_MID_LAG[i])
        zz = z + inward * jnp.where(is_end, END_OFFSET[end], MID_OFFSET[mid])
        across = jnp.where(is_end, int(end in "DEFG"), int(mid in "DEFG"))
        slot = zz * Y + jnp.where(across == 1, 1 - y, y)
        odd = lax.rem(s, 2) == 1

        def any_of(*terms):
            out = None
            for use, condition in terms:
                if use:
                    out = condition if out is None else jnp.logical_or(out, condition)
            return out

        side = any_of(
            (end in "AB", is_end),
            (end == "C", jnp.logical_and(is_end, jnp.logical_not(odd))),
            (mid in "BC", is_mid),
        )
        inner = any_of((end == "D", is_end), (mid == "A", is_mid))
        outer = any_of((mid in "BC", is_mid), (mid == "G", jnp.logical_and(is_mid, odd)))

        @pl.when(jnp.logical_and(s >= 0, s < S))
        def _():
            src = x.at[k, piece_rows(s, slot)]
            if receive:
                arrived(s, slot)
            for condition, direction in ((outer, OUTWARD), (side, SIDE), (inner, INWARD)):
                if condition is not None:
                    @pl.when(condition)
                    def _():
                        act(forward(direction, s, slot, src))
            if receive:
                to_sibling(s, slot, src).start()

    def line(s, receive, act):
        def go(j, c):
            for sign in (-1, 1):
                zz = z + sign * j

                @pl.when(jnp.logical_and(zz >= 0, zz < Z))
                def _():
                    src = x.at[k, piece_rows(s, zz)]
                    if receive:
                        arrived(s, zz)
                    toward = jnp.where(inward == -sign, INWARD, OUTWARD)
                    target = z - sign

                    @pl.when(jnp.logical_and(target >= 0, target < Z))
                    def _():
                        act(remote(
                            src, src, gsend.at[toward, s, zz], grecv.at[s, zz], target, k
                        ))
                    if receive:
                        to_sibling(s, zz, src).start()
            return c

        lax.fori_loop(1, Z, go, 0)

    if Y == 2:
        assert Z == 4
        late = max(AT_END_LAG + AT_MID_LAG)
    else:
        late = 0
    ahead = min(AHEAD, S)

    for s in range(ahead):
        own_sends(s, begin)
    for s in range(S):
        to_sibling(s, me, own_piece(s)).start()

    def low_first(i):
        return remote(
            low_out.at[feature_part(i)], wlow.at[k, feature_part(i)],
            wsend.at[i], wrecv.at[i], me, sib,
        )

    def lower(i, c):
        part = feature_part(i)
        w_copy(i).wait()
        low_out[part, :] = w[part, columns(sib)].astype(BF16)
        low_first(i).start()
        wlow[k, part, :] = w[part, columns(k)].astype(BF16)
        return c

    def meta_copy(p):
        peer = lax.rem(me + p, n)
        return remote(meta, meta_all.at[me], msend, mrecv, peer, k)

    meta_all[me] = meta[...]
    fsum[...] = jnp.zeros_like(fsum)

    active_count = active[0]
    class_base = mine * ck
    lane = lax.broadcasted_iota(jnp.int32, (LANES, LANES), 1)
    lane_float = lane.astype(F32)
    row_number = lax.broadcasted_iota(jnp.int32, (LANES, LANES), 0).astype(F32)

    def spread(row):
        return jnp.broadcast_to(row, (LANES, LANES)).T

    def share(piece, ssem, rsem, everyone):
        def copy(p):
            peer = lax.rem(mine + p, nd)
            return remote(piece, piece, ssem, rsem, peer // 2, lax.rem(peer, 2))

        def start():
            def go(p, c):
                copy(p).start()
                return c

            lax.fori_loop(1, nd, go, 0)

        def wait_in():
            remote(everyone, everyone, ssem, rsem, me, sib).wait_recv()

        def wait_out():
            remote(everyone, everyone, ssem, rsem, me, sib).wait_send()

        return start, wait_in, wait_out

    def share1(s):
        return share(
            stat1.at[s, mine], s1send.at[s], s1recv.at[s], stat1.at[s, pl.ds(0, nd - 1)]
        )

    def share2(b):
        return share(
            stat2.at[b, mine], s2send.at[b], s2recv.at[b], stat2.at[b, pl.ds(0, nd - 1)]
        )

    def exponents(base, rows, logits, with_label):
        index = class_base + lax.broadcasted_iota(jnp.int32, (rows, ck), 1)
        masked = jnp.where(index < active_count, logits, NEGATIVE)
        peak = jnp.max(masked, axis=1, keepdims=True)
        exponent = jnp.exp(masked - peak)
        total = jnp.sum(exponent, axis=1, keepdims=True)
        place = pl.ds(pl.multiple_of(base, rows), rows)
        e_scr[place, :] = exponent
        if with_label:
            target = target_col[place, 0:1]
            label = jnp.sum(
                jnp.where(index.astype(F32) == target, logits, 0.0), axis=1, keepdims=True
            )
        tile = jnp.zeros((LANES, LANES), F32)
        for j in range(rows // LANES):
            part = slice(j * LANES, (j + 1) * LANES)
            tile = jnp.where(lane == j, peak[part], tile)
            tile = jnp.where(lane == 4 + j, total[part], tile)
            if with_label:
                tile = jnp.where(lane == 8 + j, label[part], tile)
        return tile.T

    def combine(stat, b):
        peak = stat[b, 0, 0:4]
        for d in range(1, nd):
            peak = jnp.maximum(peak, stat[b, d, 0:4])
        total = jnp.zeros_like(peak)
        for d in range(nd):
            total = total + stat[b, d, 4:8] * jnp.exp(stat[b, d, 0:4] - peak)
        return peak, total, jnp.exp(stat[b, mine, 0:4] - peak) / total

    def residuals(base, rows, factor, first):
        for j in range(rows // LANES):
            place = pl.ds(pl.multiple_of(base + j * LANES, LANES), LANES)
            weight = spread(factor[j:j + 1])
            valid = valid_col[place, :]
            target = target_col[place, :]
            if first:
                square = ssq[place, :]
            for c in range(ck // LANES):
                cols = slice(c * LANES, (c + 1) * LANES)
                probability = e_scr[place, cols] * weight
                index = lane_float + (class_base + c * LANES).astype(F32)
                is_label = (index == target).astype(F32)
                r_scr[k, place, cols] = (valid * (probability - is_label)).astype(BF16)
                if first:
                    fw = (valid * probability * (1.0 - probability)).astype(BF16)
                    fw_scr[k, place, cols] = fw
                    fsum[...] += fw.astype(F32) * square

    def swap(buffer, base, rows, ssem, rsem, owner):
        place = buffer.at[owner, pl.ds(pl.multiple_of(base, rows), rows)]
        return remote(place, place, ssem, rsem, me, sib)

    def clear(i, c):
        part = feature_part(i)
        moved[part, :] = jnp.zeros((step, 2 * ck), F32)
        for h in range(2):
            inv[h, part, :] = jnp.zeros((step, ck), F32)
        return c

    def task_logits(s):
        rows = round_rows(s)
        everything = x.at[sib, rows]
        own_copy(s).wait()
        remote(everything, everything, sib_send.at[s], sib_recv.at[s], me, sib).wait_recv()

        @pl.when(s == 0)
        def _():
            def arrive(i, c):
                part = wlow.at[sib, feature_part(i)]
                remote(part, part, wsend.at[i], wrecv.at[i], me, sib).wait_recv()
                low_first(i).wait_send()
                return c

            lax.fori_loop(0, parts, arrive, 0)

            def meta_start(p, c):
                meta_copy(p).start()
                return c

            lax.fori_loop(1, n, meta_start, 0)

        logits = jnp.dot(x[0, rows, :], wlow[0], preferred_element_type=F32)
        logits = logits + jnp.dot(x[1, rows, :], wlow[1], preferred_element_type=F32)
        tile = exponents(s * per_round, per_round, logits, False)
        stat1[s, mine] = tile[0:8, :]
        share1(s)[0]()
        squares = jnp.zeros((per_round, 1), F32)
        for h in range(2):
            block = x[h, rows, :]
            squares = squares + jnp.sum((block * block).astype(F32), axis=1, keepdims=True)
        ssq[rows, :] = jnp.broadcast_to(squares, (per_round, LANES))
        xt[:, rows] = x[k, rows, :].T

    def task_residual(s):
        @pl.when(s == 0)
        def _():
            remote(
                meta_all.at[pl.ds(0, n - 1)], meta_all.at[pl.ds(0, n - 1)],
                msend, mrecv, me, sib,
            ).wait_recv()
            valid_total = meta_all[0, 1:2, :]
            for d in range(1, n):
                valid_total = valid_total + meta_all[d, 1:2, :]

            def spell(slot, c):
                target = spread(meta_all[slot, 0:1, :])
                valid = (row_number < meta_all[slot, 1:2, :]).astype(F32) / valid_total
                for t in range(S):
                    place = piece_rows(t, slot)
                    target_col[place, :] = target[t * q:(t + 1) * q]
                    valid_col[place, :] = valid[t * q:(t + 1) * q]
                return c

            lax.fori_loop(0, n, spell, 0)

        share1(s)[1]()
        factor = combine(stat1, s)[2]
        base = s * per_round
        residuals(base, per_round, factor, True)
        swap(r_scr, base, per_round, rsend.at[s], rrecv.at[s], k).start()
        swap(fw_scr, base, per_round, fsend.at[s], frecv.at[s], k).start()

    def task_gradient(s, c):
        rows = round_rows(s)

        def go(i, carry):
            part = feature_part(i)
            block = xt[part, rows]
            moved[part, columns(c)] += jnp.dot(
                block, r_scr[c, rows, :], preferred_element_type=F32
            )
            inv[c, part, :] += jnp.dot(
                block * block, fw_scr[c, rows, :], preferred_element_type=F32
            )
            return carry

        lax.fori_loop(0, parts, go, 0, unroll=2)

    def when_round(s, act):
        @pl.when(jnp.logical_and(s >= 0, s < S))
        def _():
            act(s)

    def tasks(p, at):
        r = p - late - 1
        if at == TASK_L:
            when_round(r, task_logits)
        if at == TASK_R:
            when_round(r - 1, task_residual)
        if at == TASK_OWN:
            when_round(r - 1, lambda s: task_gradient(s, k))

            @pl.when(p == 0)
            def _():
                lax.fori_loop(0, parts, clear, 0)
        if at == TASK_SIB:
            def other(s):
                base = s * per_round
                swap(r_scr, base, per_round, rsend.at[s], rrecv.at[s], sib).wait_recv()
                swap(fw_scr, base, per_round, fsend.at[s], frecv.at[s], sib).wait_recv()
                task_gradient(s, sib)

            when_round(r - 1, other)

    lax.fori_loop(0, parts, lower, 0)

    def period(p, c):
        for i in range(7):
            if i == OWN_AT:
                when_round(p + ahead, lambda s: own_sends(s, begin))
            if Y == 2:
                event(p, i, True, begin)
            elif i == 0:
                when_round(p, lambda s: line(s, True, begin))
            tasks(p, i)
        return c

    lax.fori_loop(0, S + late + 2, period, 0)

    fisher_part = jnp.sum(jnp.sum(fsum[...], axis=0, keepdims=True), axis=1, keepdims=True)
    damp_all[mine] = jnp.broadcast_to(fisher_part, damp_all.shape[1:])
    start_d, in_d, out_d = share(
        damp_all.at[mine], dsend, drecv, damp_all.at[pl.ds(0, nd - 1)]
    )
    start_d()
    e_scr[...] = jnp.zeros_like(e_scr)
    in_d()
    fisher_sum = damp_all[0, 0:1, 0:1]
    for d in range(1, nd):
        fisher_sum = fisher_sum + damp_all[d, 0:1, 0:1]
    damping = DAMPING_SHARE * fisher_sum / scale + EPSILON

    def update(i, c):
        part = feature_part(i)
        inverse = 1.0 / (inv[c, part, :] + damping)
        inv[c, part, :] = inverse
        change = moved[part, columns(c)] * inverse
        moved[part, columns(c)] = change
        return (w[part, columns(c)] - LEARNING_RATE * change).astype(BF16)

    def low_second(i):
        return remote(
            low_out.at[feature_part(i)], wlow.at[k, feature_part(i)],
            lsend.at[i], lrecv.at[i], me, sib,
        )

    def update_other(i, c):
        low_out[feature_part(i), :] = update(i, sib)
        low_second(i).start()
        return c

    lax.fori_loop(0, parts, update_other, 0)

    def update_own(i, c):
        part = feature_part(i)
        low = update(i, k)
        e_scr[...] += jnp.dot(x[k, :, part], low, preferred_element_type=F32)
        return c

    lax.fori_loop(0, parts, update_own, 0)

    def low_arrive(i, c):
        part = wlow.at[sib, feature_part(i)]
        remote(part, part, lsend.at[i], lrecv.at[i], me, sib).wait_recv()
        return c

    lax.fori_loop(0, parts, low_arrive, 0)

    def rounds_out(s, c):
        swap(r_scr, s * per_round, per_round, rsend.at[s], rrecv.at[s], k).wait_send()
        swap(fw_scr, s * per_round, per_round, fsend.at[s], frecv.at[s], k).wait_send()
        return c

    lax.fori_loop(0, S, rounds_out, 0)

    def second(b, c):
        rows = pl.ds(pl.multiple_of(b * HALF_ROWS, HALF_ROWS), HALF_ROWS)
        logits = e_scr[rows, :] + jnp.dot(
            x[sib, rows, :], wlow[sib], preferred_element_type=F32
        )
        tile = exponents(b * HALF_ROWS, HALF_ROWS, logits, True)
        stat2[b, mine] = tile[0:16, :]
        share2(b)[0]()
        return c

    lax.fori_loop(0, halves, second, 0)

    def swap2(b, owner):
        return swap(r_scr, b * HALF_ROWS, HALF_ROWS, r2send.at[b], r2recv.at[b], owner)

    def last(b, c):
        rows = pl.ds(pl.multiple_of(b * HALF_ROWS, HALF_ROWS), HALF_ROWS)
        sign = jnp.where(b == 0, -1.0, 1.0).astype(F32)
        share2(b)[1]()
        peak, total, factor = combine(stat2, b)
        residuals(b * HALF_ROWS, HALF_ROWS, factor, False)
        swap2(b, k).start()
        label = stat2[b, 0, 8:12]
        for d in range(1, nd):
            label = label + stat2[b, d, 8:12]
        loss = peak + jnp.log(total) - label
        for j in range(per_half):
            loss_col[pl.ds(pl.multiple_of(b * HALF_ROWS + j * LANES, LANES), LANES), :] = (
                spread(loss[j:j + 1])
            )

        def gradient(owner):
            def go(i, carry):
                part = feature_part(i)
                grad = jnp.dot(xt[part, rows], r_scr[owner, rows, :], preferred_element_type=F32)
                moved[part, columns(owner)] = (
                    sign * moved[part, columns(owner)] - grad * inv[owner, part, :]
                )
                return carry

            lax.fori_loop(0, parts, go, 0, unroll=2)

        gradient(k)
        swap2(b, sib).wait_recv()
        gradient(sib)
        return c

    lax.fori_loop(0, halves, last, 0)

    own = jnp.concatenate([loss_col[piece_rows(s, me), :] for s in range(S)], axis=0).T
    losses[...] = (lane_float[0:1] < meta[1:2, :]).astype(F32) * own[0:1, :]

    def drain(p, c):
        when_round(p, lambda s: own_sends(s, finish))
        if Y == 2:
            for i in range(7):
                event(p, i, False, finish)
        else:
            when_round(p, lambda s: line(s, False, finish))

        def rest(s):
            everything = x.at[k, round_rows(s)]
            remote(
                everything, everything, sib_send.at[s], sib_recv.at[s], me, sib
            ).wait_send()
            share1(s)[2]()

        when_round(p, rest)
        return c

    lax.fori_loop(0, S + late, drain, 0)
    remote(
        meta_all.at[pl.ds(0, n - 1)], meta_all.at[pl.ds(0, n - 1)], msend, mrecv, me, sib
    ).wait_send()
    out_d()

    def parts_out(i, c):
        low_second(i).wait_send()
        return c

    lax.fori_loop(0, parts, parts_out, 0)

    def halves_out(b, c):
        share2(b)[2]()
        swap2(b, k).wait_send()
        return c

    lax.fori_loop(0, halves, halves_out, 0)


def solution(mesh):
    n = mesh.shape["example"]
    Y = 2 if n == 8 else 1
    Z = n // Y
    nd = 2 * n

    def body(features, weights, labels, counts, active):
        rows_n, half = features.shape
        local = weights.shape[1]
        ck = local // 2
        all_rows = rows_n * n
        halves = all_rows // HALF_ROWS
        target = (labels % active[0]).astype(F32)
        meta = jnp.concatenate(
            [
                target[None, :],
                jnp.broadcast_to(counts.astype(F32)[:, None], (7, rows_n)),
            ],
            axis=0,
        )
        scale = float(half * 2 * local * n)
        parts = half // min(512, half)
        dma = pltpu.SemaphoreType.DMA
        moved, losses = pl.pallas_call(
            functools.partial(kernel, Z, Y, scale),
            out_shape=(
                pltpu.VMEM(weights.shape, F32),
                jax.ShapeDtypeStruct((1, rows_n), F32),
            ),
            in_specs=[
                pl.BlockSpec(memory_space=pl.ANY),
                pl.BlockSpec(memory_space=pl.ANY),
                pl.BlockSpec(memory_space=pltpu.VMEM),
                pl.BlockSpec(memory_space=pltpu.SMEM),
            ],
            out_specs=(
                pl.BlockSpec(memory_space=pltpu.VMEM),
                pl.BlockSpec(memory_space=pltpu.VMEM),
            ),
            scratch_shapes=[
                pltpu.VMEM((2, all_rows, half), BF16),
                pltpu.VMEM((half, all_rows), BF16),
                pltpu.VMEM((half, local), F32),
                pltpu.VMEM((2, half, ck), BF16),
                pltpu.VMEM((half, ck), BF16),
                pltpu.VMEM((all_rows, ck), F32),
                pltpu.VMEM((2, all_rows, ck), BF16),
                pltpu.VMEM((2, all_rows, ck), BF16),
                pltpu.VMEM((2, half, ck), F32),
                pltpu.VMEM((n, 8, rows_n), F32),
                pltpu.VMEM((all_rows, LANES), F32),
                pltpu.VMEM((all_rows, LANES), F32),
                pltpu.VMEM((all_rows, LANES), F32),
                pltpu.VMEM((LANES, LANES), F32),
                pltpu.VMEM((ROUNDS, nd, 8, LANES), F32),
                pltpu.VMEM((halves, nd, 16, LANES), F32),
                pltpu.VMEM((nd, 8, LANES), F32),
                pltpu.VMEM((all_rows, LANES), F32),
                dma((ROUNDS,)), dma((parts,)),
                dma((3, ROUNDS, n)), dma((ROUNDS, n)),
                dma((ROUNDS,)), dma((ROUNDS,)),
                dma((parts,)), dma((parts,)), dma((parts,)), dma((parts,)),
                dma, dma,
                dma((ROUNDS,)), dma((ROUNDS,)), dma((halves,)), dma((halves,)), dma, dma,
                dma((ROUNDS,)), dma((ROUNDS,)), dma((ROUNDS,)), dma((ROUNDS,)),
                dma((halves,)), dma((halves,)),
            ],
            compiler_params=pltpu.CompilerParams(
                collective_id=0, has_side_effects=True, vmem_limit_bytes=57671680
            ),
        )(features, weights, meta, active)
        return moved, losses.reshape(rows_n)

    return jax.shard_map(
        body,
        mesh=mesh,
        in_specs=(
            P(("groups", "example"), "cls"),
            P(("groups", "cls"), "example"),
            P(("groups", "example")),
            P(("groups", "example")),
            P("groups"),
        ),
        out_specs=(P(("groups", "cls"), "example"), P(("groups", "example"))),
        check_vma=False,
    )
```

```python
import functools

import jax
import jax.numpy as jnp
from jax import lax
from jax.experimental import pallas as pl
from jax.experimental.pallas import tpu as pltpu
from jax.sharding import PartitionSpec as P

NEGATIVE = -1e30
LEARNING_RATE = 2e-05
DAMPING_SHARE = 0.1
EPSILON = 1e-06
MESH = pl.DeviceIdType.MESH
INWARD, OUTWARD, SIDE = 0, 1, 2
F32, BF16 = jnp.float32, jnp.bfloat16

ROUNDS = 4
LANES = 128
HALF_ROWS = 512
AHEAD = 3
OWN_AT = 2
AT_END = "DCEAFBG"
AT_END_LAG = (0, 1, 1, 0, 1, 0, 1)
AT_MID = "ABEGDFC"
AT_MID_LAG = (0, 0, 1, 1, 0, 1, 0)
END_OFFSET = dict(A=1, B=2, C=3, D=0, E=1, F=2, G=3)
MID_OFFSET = dict(A=-1, B=1, C=2, D=0, E=1, F=-1, G=2)
TASK_L, TASK_R, TASK_OWN, TASK_SIB = 0, 1, 3, 3


def kernel(
    Z, Y, scale,
    features, weights, labels, counts, active,
    moved, losses,
    x, xt, w, wlow, low_out, e_scr, r_scr, fw_scr, inv,
    meta_all, target_col, valid_col, ssq, fsum, stat1, stat2, damp_all, labels_all, loss_row, loss_col,
    own_sem, w_sem, gsend, grecv, sib_send, sib_recv,
    wsend, wrecv, lsend, lrecv, msend, mrecv,
    s1send, s1recv, s2send, s2recv, dsend, drecv,
    rsend, rrecv, fsend, frecv, r2send, r2recv,
):
    n = Z * Y
    nd = 2 * n
    rows_n, half = features.shape
    S = ROUNDS
    q = rows_n // S
    per_round = n * q
    groups = per_round // LANES
    all_rows = n * rows_n
    ck = moved.shape[1] // 2
    step = min(512, half)
    parts = half // step
    halves = all_rows // HALF_ROWS
    per_half = HALF_ROWS // LANES
    me = lax.axis_index("example")
    k = lax.axis_index("cls")
    sib = 1 - k
    z, y = me // Y, lax.rem(me, Y)
    mine = me * 2 + k
    inward = jnp.where(z < Z // 2, 1, -1)
    is_end = jnp.logical_or(z == 0, z == Z - 1)
    is_mid = jnp.logical_not(is_end)

    def round_rows(s):
        return pl.ds(pl.multiple_of(s * per_round, per_round), per_round)

    def piece_rows(s, slot):
        return pl.ds(pl.multiple_of(s * per_round + slot * q, q), q)

    def columns(c):
        return pl.ds(pl.multiple_of(c * ck, ck), ck)

    def feature_part(i):
        return pl.ds(pl.multiple_of(i * step, step), step)

    def remote(src, dst, ssem, rsem, example, core):
        return pltpu.make_async_remote_copy(
            src_ref=src, dst_ref=dst, send_sem=ssem, recv_sem=rsem,
            device_id={"example": example, "cls": core}, device_id_type=MESH,
        )

    def own_piece(s):
        return features.at[pl.ds(pl.multiple_of(s * q, q), q)]

    def own_copy(s):
        return pltpu.make_async_copy(own_piece(s), x.at[k, piece_rows(s, me)], own_sem.at[s])

    def w_copy(i):
        return pltpu.make_async_copy(
            weights.at[feature_part(i)], w.at[feature_part(i)], w_sem.at[i]
        )

    for s in range(S):
        own_copy(s).start()
    for i in range(parts):
        w_copy(i).start()

    barrier = pltpu.get_barrier_semaphore()

    def greet(example, core):
        pl.semaphore_signal(
            barrier, inc=1, device_id={"example": example, "cls": core}, device_id_type=MESH
        )

    greet(me, sib)
    if Y == 2:
        greet(z * Y + (1 - y), k)

    @pl.when(z < Z - 1)
    def _():
        greet(me + Y, k)

    @pl.when(z > 0)
    def _():
        greet(me - Y, k)

    pl.semaphore_wait(barrier, Y + (z < Z - 1).astype(jnp.int32) + (z > 0).astype(jnp.int32))

    def forward(direction, s, slot, src):
        target = {
            INWARD: me + inward * Y,
            OUTWARD: me - inward * Y,
            SIDE: z * Y + (Y - 1 - y),
        }[direction]
        return remote(
            src, x.at[k, piece_rows(s, slot)], gsend.at[direction, s, slot],
            grecv.at[s, slot], target, k,
        )

    def to_sibling(s, slot, src):
        return remote(
            src, x.at[k, piece_rows(s, slot)], sib_send.at[s], sib_recv.at[s], me, sib
        )

    def arrived(s, slot):
        place = x.at[k, piece_rows(s, slot)]
        remote(place, place, gsend.at[SIDE, s, slot], grecv.at[s, slot], me, sib).wait_recv()

    def has_outer():
        return jnp.logical_and(z - inward >= 0, z - inward < Z)

    def own_sends(s, act):
        src = own_piece(s)
        act(forward(INWARD, s, me, src))

        @pl.when(has_outer())
        def _():
            act(forward(OUTWARD, s, me, src))

        if Y == 2:
            act(forward(SIDE, s, me, src))

    def begin(copy):
        copy.start()

    def finish(copy):
        copy.wait_send()

    def event(p, i, receive, act):
        end, mid = AT_END[i], AT_MID[i]
        s = p - jnp.where(is_end, AT_END_LAG[i], AT_MID_LAG[i])
        zz = z + inward * jnp.where(is_end, END_OFFSET[end], MID_OFFSET[mid])
        across = jnp.where(is_end, int(end in "DEFG"), int(mid in "DEFG"))
        slot = zz * Y + jnp.where(across == 1, 1 - y, y)
        odd = lax.rem(s, 2) == 1

        def any_of(*terms):
            out = None
            for use, condition in terms:
                if use:
                    out = condition if out is None else jnp.logical_or(out, condition)
            return out

        side = any_of(
            (end in "AB", is_end),
            (end == "C", jnp.logical_and(is_end, jnp.logical_not(odd))),
            (mid in "BC", is_mid),
        )
        inner = any_of((end == "D", is_end), (mid == "A", is_mid))
        outer = any_of((mid in "BC", is_mid), (mid == "G", jnp.logical_and(is_mid, odd)))

        @pl.when(jnp.logical_and(s >= 0, s < S))
        def _():
            src = x.at[k, piece_rows(s, slot)]
            if receive:
                arrived(s, slot)
            for condition, direction in ((outer, OUTWARD), (side, SIDE), (inner, INWARD)):
                if condition is not None:
                    @pl.when(condition)
                    def _():
                        act(forward(direction, s, slot, src))
            if receive:
                to_sibling(s, slot, src).start()

    def line(s, receive, act):
        def go(j, c):
            for sign in (-1, 1):
                zz = z + sign * j

                @pl.when(jnp.logical_and(zz >= 0, zz < Z))
                def _():
                    src = x.at[k, piece_rows(s, zz)]
                    if receive:
                        arrived(s, zz)
                    toward = jnp.where(inward == -sign, INWARD, OUTWARD)
                    target = z - sign

                    @pl.when(jnp.logical_and(target >= 0, target < Z))
                    def _():
                        act(remote(
                            src, src, gsend.at[toward, s, zz], grecv.at[s, zz], target, k
                        ))
                    if receive:
                        to_sibling(s, zz, src).start()
            return c

        lax.fori_loop(1, Z, go, 0)

    if Y == 2:
        assert Z == 4
        late = max(AT_END_LAG + AT_MID_LAG)
    else:
        late = 0
    ahead = min(AHEAD, S)

    for s in range(ahead):
        own_sends(s, begin)
    for s in range(S):
        to_sibling(s, me, own_piece(s)).start()

    def low_first(i):
        return remote(
            low_out.at[feature_part(i)], wlow.at[k, feature_part(i)],
            wsend.at[i], wrecv.at[i], me, sib,
        )

    def lower(i, c):
        part = feature_part(i)
        w_copy(i).wait()
        low_out[part, :] = w[part, columns(sib)].astype(BF16)
        low_first(i).start()
        wlow[k, part, :] = w[part, columns(k)].astype(BF16)
        return c

    def meta_copy(p):
        peer = lax.rem(me + p, n)
        return remote(meta_all.at[me], meta_all.at[me], msend, mrecv, peer, k)

    count = counts[0].astype(F32)
    label = labels[...]
    target_row = jnp.where(label >= active[0], label - active[0], label).astype(F32)
    meta_row = lax.broadcasted_iota(jnp.int32, (8, rows_n), 0)
    meta_all[me] = jnp.where(meta_row == 0, jnp.broadcast_to(target_row, (8, rows_n)), count)
    fsum[...] = jnp.zeros_like(fsum)

    active_count = active[0]
    class_base = mine * ck
    lane = lax.broadcasted_iota(jnp.int32, (LANES, LANES), 1)
    lane_float = lane.astype(F32)
    row_number = lax.broadcasted_iota(jnp.int32, (LANES, LANES), 0).astype(F32)

    def spread(row):
        return jnp.broadcast_to(row, (LANES, LANES)).T

    def share(piece, ssem, rsem, everyone):
        def copy(p):
            peer = lax.rem(mine + p, nd)
            return remote(piece, piece, ssem, rsem, peer // 2, lax.rem(peer, 2))

        def start():
            def go(p, c):
                copy(p).start()
                return c

            lax.fori_loop(1, nd, go, 0)

        def wait_in():
            remote(everyone, everyone, ssem, rsem, me, sib).wait_recv()

        def wait_out():
            remote(everyone, everyone, ssem, rsem, me, sib).wait_send()

        return start, wait_in, wait_out

    def share1(s):
        return share(
            stat1.at[s, mine], s1send.at[s], s1recv.at[s], stat1.at[s, pl.ds(0, nd - 1)]
        )

    def share2(b):
        return share(
            stat2.at[b, mine], s2send.at[b], s2recv.at[b], stat2.at[b, pl.ds(0, nd - 1)]
        )

    def exponents(base, rows, logits, with_label):
        index = class_base + lax.broadcasted_iota(jnp.int32, (rows, ck), 1)
        masked = jnp.where(index < active_count, logits, NEGATIVE)
        peak = jnp.max(masked, axis=1, keepdims=True)
        exponent = jnp.exp(masked - peak)
        total = jnp.sum(exponent, axis=1, keepdims=True)
        place = slice(base, base + rows) if isinstance(base, int) else pl.ds(pl.multiple_of(base, rows), rows)
        e_scr[place, :] = exponent
        if with_label:
            target = target_col[place, 0:1]
            label = jnp.sum(
                jnp.where(index.astype(F32) == target, logits, 0.0), axis=1, keepdims=True
            )
        count_rows = rows // LANES
        tile = jnp.zeros((LANES, LANES), F32)
        for j in range(count_rows):
            part = slice(j * LANES, (j + 1) * LANES)
            tile = jnp.where(lane == j, peak[part], tile)
            tile = jnp.where(lane == count_rows + j, total[part], tile)
            if with_label:
                tile = jnp.where(lane == 2 * count_rows + j, label[part], tile)
        return tile.T

    def combine(stat, b):
        count_rows = stat.shape[2] // 2
        tops, sums = slice(0, count_rows), slice(count_rows, 2 * count_rows)
        peak = stat[b, 0, tops]
        for d in range(1, nd):
            peak = jnp.maximum(peak, stat[b, d, tops])
        total = jnp.zeros_like(peak)
        for d in range(nd):
            total = total + stat[b, d, sums] * jnp.exp(stat[b, d, tops] - peak)
        return peak, total, jnp.exp(stat[b, mine, tops] - peak) / total

    def residuals(base, rows, factor, first):
        for j in range(rows // LANES):
            place = pl.ds(pl.multiple_of(base + j * LANES, LANES), LANES)
            weight = spread(factor[j:j + 1])
            valid = valid_col[place, :]
            target = target_col[place, :]
            if first:
                square = ssq[place, :]
            for c in range(ck // LANES):
                cols = slice(c * LANES, (c + 1) * LANES)
                probability = e_scr[place, cols] * weight
                index = lane_float + (class_base + c * LANES).astype(F32)
                is_label = (index == target).astype(F32)
                r_scr[k, place, cols] = (valid * (probability - is_label)).astype(BF16)
                if first:
                    fw = (valid * probability * (1.0 - probability)).astype(BF16)
                    fw_scr[k, place, cols] = fw
                    fsum[...] += fw.astype(F32) * square

    def swap(buffer, base, rows, ssem, rsem, owner):
        place = buffer.at[owner, pl.ds(pl.multiple_of(base, rows), rows)]
        return remote(place, place, ssem, rsem, me, sib)

    def clear(i, c):
        part = feature_part(i)
        moved[part, :] = jnp.zeros((step, 2 * ck), F32)
        for h in range(2):
            inv[h, part, :] = jnp.zeros((step, ck), F32)
        return c

    def task_logits(s):
        rows = round_rows(s)
        everything = x.at[sib, rows]
        own_copy(s).wait()
        remote(everything, everything, sib_send.at[s], sib_recv.at[s], me, sib).wait_recv()

        @pl.when(s == 0)
        def _():
            def arrive(i, c):
                part = wlow.at[sib, feature_part(i)]
                remote(part, part, wsend.at[i], wrecv.at[i], me, sib).wait_recv()
                low_first(i).wait_send()
                return c

            lax.fori_loop(0, parts, arrive, 0)

            def meta_start(p, c):
                meta_copy(p).start()
                return c

            lax.fori_loop(1, n, meta_start, 0)

        logits = jnp.dot(x[0, rows, :], wlow[0], preferred_element_type=F32)
        logits = logits + jnp.dot(x[1, rows, :], wlow[1], preferred_element_type=F32)
        tile = exponents(s * per_round, per_round, logits, False)
        stat1[s, mine] = tile[0:2 * groups, :]
        share1(s)[0]()
        squares = jnp.zeros((per_round, 1), F32)
        for h in range(2):
            block = x[h, rows, :]
            squares = squares + jnp.sum((block * block).astype(F32), axis=1, keepdims=True)
        ssq[rows, :] = jnp.broadcast_to(squares, (per_round, LANES))
        xt[:, rows] = x[k, rows, :].T

    start_d, in_d, out_d = share(
        damp_all.at[mine], dsend.at[0], drecv.at[0], damp_all.at[pl.ds(0, nd - 1)]
    )

    def task_residual(s):
        @pl.when(s == 0)
        def _():
            remote(
                meta_all.at[pl.ds(0, n - 1)], meta_all.at[pl.ds(0, n - 1)],
                msend, mrecv, me, sib,
            ).wait_recv()
            valid_total = meta_all[0, 1:2, :]
            for d in range(1, n):
                valid_total = valid_total + meta_all[d, 1:2, :]

            def spell(slot, c):
                target = spread(meta_all[slot, 0:1, :])
                valid = (row_number < meta_all[slot, 1:2, :]).astype(F32) / valid_total
                for t in range(S):
                    place = piece_rows(t, slot)
                    target_col[place, :] = target[t * q:(t + 1) * q]
                    valid_col[place, :] = valid[t * q:(t + 1) * q]
                return c

            lax.fori_loop(0, n, spell, 0)

        share1(s)[1]()
        factor = combine(stat1, s)[2]
        base = s * per_round
        residuals(base, per_round, factor, True)
        swap(r_scr, base, per_round, rsend.at[s], rrecv.at[s], k).start()
        swap(fw_scr, base, per_round, fsend.at[s], frecv.at[s], k).start()

        @pl.when(s == S - 1)
        def _():
            part = jnp.sum(jnp.sum(fsum[...], axis=0, keepdims=True), axis=1, keepdims=True)
            damp_all[mine] = jnp.broadcast_to(part, damp_all.shape[1:])
            start_d()

    def task_gradient(s, c):
        rows = round_rows(s)

        def go(i, carry):
            part = feature_part(i)
            block = xt[part, rows]
            moved[part, columns(c)] += jnp.dot(
                block, r_scr[c, rows, :], preferred_element_type=F32
            )
            inv[c, part, :] += jnp.dot(
                block * block, fw_scr[c, rows, :], preferred_element_type=F32
            )
            return carry

        lax.fori_loop(0, parts, go, 0, unroll=2)

    def when_round(s, act):
        @pl.when(jnp.logical_and(s >= 0, s < S))
        def _():
            act(s)

    def tasks(p, at):
        r = p - late - 1
        if at == TASK_L:
            when_round(r, task_logits)
        if at == TASK_R:
            when_round(r - 1, task_residual)
        if at == TASK_OWN:
            when_round(r - 1, lambda s: task_gradient(s, k))

            @pl.when(p == 0)
            def _():
                lax.fori_loop(0, parts, clear, 0)
        if at == TASK_SIB:
            def other(s):
                base = s * per_round
                swap(r_scr, base, per_round, rsend.at[s], rrecv.at[s], sib).wait_recv()
                swap(fw_scr, base, per_round, fsend.at[s], frecv.at[s], sib).wait_recv()
                task_gradient(s, sib)

            when_round(r - 1, other)

    lax.fori_loop(0, parts, lower, 0)

    def period(p, c):
        for i in range(7):
            if i == OWN_AT:
                when_round(p + ahead, lambda s: own_sends(s, begin))
            if Y == 2:
                event(p, i, True, begin)
            elif i == 0:
                when_round(p, lambda s: line(s, True, begin))
            tasks(p, i)
        return c

    lax.fori_loop(0, S + late + 2, period, 0)

    in_d()
    fisher_sum = damp_all[0, 0:1, 0:1]
    for d in range(1, nd):
        fisher_sum = fisher_sum + damp_all[d, 0:1, 0:1]
    damping = DAMPING_SHARE * fisher_sum / scale + EPSILON

    def update(i, c):
        part = feature_part(i)
        inverse = 1.0 / (inv[c, part, :] + damping)
        inv[c, part, :] = inverse
        change = moved[part, columns(c)] * inverse
        moved[part, columns(c)] = change
        return (w[part, columns(c)] - LEARNING_RATE * change).astype(BF16)

    def low_second(i):
        return remote(
            low_out.at[feature_part(i)], wlow.at[k, feature_part(i)],
            lsend.at[i], lrecv.at[i], me, sib,
        )

    def update_both(i):
        part = feature_part(i)
        low_out[part, :] = update(i, sib)
        low_second(i).start()
        low = update(i, k)
        term = jnp.dot(x[k, :, part], low, preferred_element_type=F32)
        if i == 0:
            e_scr[...] = term
        else:
            e_scr[...] += term

    for i in range(parts):
        update_both(i)

    def low_arrive(i, c):
        part = wlow.at[sib, feature_part(i)]
        remote(part, part, lsend.at[i], lrecv.at[i], me, sib).wait_recv()
        return c

    lax.fori_loop(0, parts, low_arrive, 0)

    def rounds_out(s, c):
        swap(r_scr, s * per_round, per_round, rsend.at[s], rrecv.at[s], k).wait_send()
        swap(fw_scr, s * per_round, per_round, fsend.at[s], frecv.at[s], k).wait_send()
        return c

    lax.fori_loop(0, S, rounds_out, 0)

    def logits_second(b):
        rows = slice(b * HALF_ROWS, (b + 1) * HALF_ROWS)
        return e_scr[rows, :] + jnp.dot(
            x[sib, rows, :], wlow[sib], preferred_element_type=F32
        )

    logits = logits_second(0)
    for b in range(halves):
        later = logits_second(b + 1) if b + 1 < halves else None
        tile = exponents(b * HALF_ROWS, HALF_ROWS, logits, True)
        stat2[b, mine] = tile[0:2 * per_half, :]
        labels_all[mine, b * per_half:(b + 1) * per_half, :] = tile[2 * per_half:3 * per_half, :]
        share2(b)[0]()
        logits = later

    start_l, in_l, out_l = share(
        labels_all.at[mine], dsend.at[1], drecv.at[1], labels_all.at[pl.ds(0, nd - 1)]
    )
    start_l()

    def swap2(b, owner):
        return swap(r_scr, b * HALF_ROWS, HALF_ROWS, r2send.at[b], r2recv.at[b], owner)

    def last(b, c):
        rows = pl.ds(pl.multiple_of(b * HALF_ROWS, HALF_ROWS), HALF_ROWS)
        sign = jnp.where(b == 0, -1.0, 1.0).astype(F32)
        share2(b)[1]()
        peak, total, factor = combine(stat2, b)
        residuals(b * HALF_ROWS, HALF_ROWS, factor, False)
        swap2(b, k).start()
        loss_row[b] = peak + jnp.log(total)

        def gradient(owner):
            def go(i, carry):
                part = feature_part(i)
                grad = jnp.dot(xt[part, rows], r_scr[owner, rows, :], preferred_element_type=F32)
                moved[part, columns(owner)] = (
                    sign * moved[part, columns(owner)] - grad * inv[owner, part, :]
                )
                return carry

            lax.fori_loop(0, parts, go, 0, unroll=2)

        gradient(k)
        swap2(b, sib).wait_recv()
        gradient(sib)
        return c

    lax.fori_loop(0, halves, last, 0)

    in_l()

    for b in range(halves):
        names = slice(b * per_half, (b + 1) * per_half)
        label = labels_all[0, names, :]
        for d in range(1, nd):
            label = label + labels_all[d, names, :]
        loss = loss_row[b] - label
        for j in range(per_half):
            at = b * HALF_ROWS + j * LANES
            loss_col[at:at + LANES, :] = spread(loss[j:j + 1])
    own = jnp.concatenate([loss_col[piece_rows(s, me), :] for s in range(S)], axis=0).T
    losses[...] = (lane_float[0:1] < count).astype(F32) * own[0:1, :]

    def drain(p, c):
        when_round(p, lambda s: own_sends(s, finish))
        if Y == 2:
            for i in range(7):
                event(p, i, False, finish)
        else:
            when_round(p, lambda s: line(s, False, finish))

        def rest(s):
            everything = x.at[k, round_rows(s)]
            remote(
                everything, everything, sib_send.at[s], sib_recv.at[s], me, sib
            ).wait_send()
            share1(s)[2]()

        when_round(p, rest)
        return c

    lax.fori_loop(0, S + late, drain, 0)
    remote(
        meta_all.at[pl.ds(0, n - 1)], meta_all.at[pl.ds(0, n - 1)], msend, mrecv, me, sib
    ).wait_send()
    out_d()
    out_l()

    def parts_out(i, c):
        low_second(i).wait_send()
        return c

    lax.fori_loop(0, parts, parts_out, 0)

    def halves_out(b, c):
        share2(b)[2]()
        swap2(b, k).wait_send()
        return c

    lax.fori_loop(0, halves, halves_out, 0)


def solution(mesh):
    n = mesh.shape["example"]
    Y = 2 if n == 8 else 1
    Z = n // Y
    nd = 2 * n

    def body(features, weights, labels, counts, active):
        rows_n, half = features.shape
        local = weights.shape[1]
        ck = local // 2
        all_rows = rows_n * n
        halves = all_rows // HALF_ROWS
        scale = float(half * 2 * local * n)
        parts = half // min(512, half)
        dma = pltpu.SemaphoreType.DMA
        moved, losses = pl.pallas_call(
            functools.partial(kernel, Z, Y, scale),
            out_shape=(
                pltpu.VMEM(weights.shape, F32),
                jax.ShapeDtypeStruct((1, rows_n), F32),
            ),
            in_specs=[
                pl.BlockSpec(memory_space=pl.ANY),
                pl.BlockSpec(memory_space=pl.ANY),
                pl.BlockSpec(memory_space=pltpu.VMEM),
                pl.BlockSpec(memory_space=pltpu.SMEM),
                pl.BlockSpec(memory_space=pltpu.SMEM),
            ],
            out_specs=(
                pl.BlockSpec(memory_space=pltpu.VMEM),
                pl.BlockSpec(memory_space=pltpu.VMEM),
            ),
            scratch_shapes=[
                pltpu.VMEM((2, all_rows, half), BF16),
                pltpu.VMEM((half, all_rows), BF16),
                pltpu.VMEM((half, local), F32),
                pltpu.VMEM((2, half, ck), BF16),
                pltpu.VMEM((half, ck), BF16),
                pltpu.VMEM((all_rows, ck), F32),
                pltpu.VMEM((2, all_rows, ck), BF16),
                pltpu.VMEM((2, all_rows, ck), BF16),
                pltpu.VMEM((2, half, ck), F32),
                pltpu.VMEM((n, 8, rows_n), F32),
                pltpu.VMEM((all_rows, LANES), F32),
                pltpu.VMEM((all_rows, LANES), F32),
                pltpu.VMEM((all_rows, LANES), F32),
                pltpu.VMEM((LANES, LANES), F32),
                pltpu.VMEM((ROUNDS, nd, 2 * (all_rows // ROUNDS // LANES), LANES), F32),
                pltpu.VMEM((halves, nd, 2 * (HALF_ROWS // LANES), LANES), F32),
                pltpu.VMEM((nd, 1, LANES), F32),
                pltpu.VMEM((nd, all_rows // LANES, LANES), F32),
                pltpu.VMEM((halves, HALF_ROWS // LANES, LANES), F32),
                pltpu.VMEM((all_rows, LANES), F32),
                dma((ROUNDS,)), dma((parts,)),
                dma((3, ROUNDS, n)), dma((ROUNDS, n)),
                dma((ROUNDS,)), dma((ROUNDS,)),
                dma((parts,)), dma((parts,)), dma((parts,)), dma((parts,)),
                dma, dma,
                dma((ROUNDS,)), dma((ROUNDS,)), dma((halves,)), dma((halves,)), dma((2,)), dma((2,)),
                dma((ROUNDS,)), dma((ROUNDS,)), dma((ROUNDS,)), dma((ROUNDS,)),
                dma((halves,)), dma((halves,)),
            ],
            compiler_params=pltpu.CompilerParams(
                collective_id=0, has_side_effects=True, vmem_limit_bytes=57671680
            ),
        )(features, weights, labels.reshape(1, rows_n), counts, active)
        return moved, losses.reshape(rows_n)

    return jax.shard_map(
        body,
        mesh=mesh,
        in_specs=(
            P(("groups", "example"), "cls"),
            P(("groups", "cls"), "example"),
            P(("groups", "example")),
            P(("groups", "example")),
            P("groups"),
        ),
        out_specs=(P(("groups", "cls"), "example"), P(("groups", "example"))),
        check_vma=False,
    )
```

```python
import functools

import jax
import jax.numpy as jnp
from jax import lax
from jax.experimental import pallas as pl
from jax.experimental.pallas import tpu as pltpu
from jax.sharding import PartitionSpec as P

NEGATIVE = -1e30
LEARNING_RATE = 2e-05
DAMPING_SHARE = 0.1
EPSILON = 1e-06
MESH = pl.DeviceIdType.MESH
INWARD, OUTWARD, SIDE = 0, 1, 2
F32, BF16 = jnp.float32, jnp.bfloat16

ROUNDS = 4
LANES = 128
HALF_ROWS = 512
AHEAD = 3
OWN_AT = 2
AT_END = "DCEAFBG"
AT_END_LAG = (0, 1, 1, 0, 1, 0, 1)
AT_MID = "ABEGDFC"
AT_MID_LAG = (0, 0, 1, 1, 0, 1, 0)
END_OFFSET = dict(A=1, B=2, C=3, D=0, E=1, F=2, G=3)
MID_OFFSET = dict(A=-1, B=1, C=2, D=0, E=1, F=-1, G=2)
TASK_L, TASK_R, TASK_OWN, TASK_SIB = 0, 4, 5, 6


def kernel(
    Z, Y, scale,
    features, weights, labels, counts, active,
    moved, losses,
    x, xt, w, wlow, low_out, e_scr, r_scr, fw_scr, inv,
    meta_all, target_col, valid_col, ssq, fsum, stat1, stat2, damp_all, labels_all, loss_row, loss_col,
    own_sem, w_sem, gsend, grecv, sib_send, sib_recv,
    wsend, wrecv, lsend, lrecv, msend, mrecv,
    s1send, s1recv, s2send, s2recv, dsend, drecv,
    rsend, rrecv, fsend, frecv, r2send, r2recv,
):
    n = Z * Y
    nd = 2 * n
    rows_n, half = features.shape
    S = ROUNDS
    q = rows_n // S
    per_round = n * q
    groups = per_round // LANES
    all_rows = n * rows_n
    ck = moved.shape[1] // 2
    step = min(512, half)
    parts = half // step
    halves = all_rows // HALF_ROWS
    per_half = HALF_ROWS // LANES
    me = lax.axis_index("example")
    k = lax.axis_index("cls")
    sib = 1 - k
    z, y = me // Y, lax.rem(me, Y)
    mine = me * 2 + k
    inward = jnp.where(z < Z // 2, 1, -1)
    is_end = jnp.logical_or(z == 0, z == Z - 1)
    is_mid = jnp.logical_not(is_end)

    def round_rows(s):
        return pl.ds(pl.multiple_of(s * per_round, per_round), per_round)

    def piece_rows(s, slot):
        return pl.ds(pl.multiple_of(s * per_round + slot * q, q), q)

    def columns(c):
        return pl.ds(pl.multiple_of(c * ck, ck), ck)

    def feature_part(i):
        return pl.ds(pl.multiple_of(i * step, step), step)

    def remote(src, dst, ssem, rsem, example, core):
        return pltpu.make_async_remote_copy(
            src_ref=src, dst_ref=dst, send_sem=ssem, recv_sem=rsem,
            device_id={"example": example, "cls": core}, device_id_type=MESH,
        )

    def own_piece(s):
        return features.at[pl.ds(pl.multiple_of(s * q, q), q)]

    def own_copy(s):
        return pltpu.make_async_copy(own_piece(s), x.at[k, piece_rows(s, me)], own_sem.at[s])

    def w_copy(i):
        return pltpu.make_async_copy(
            weights.at[feature_part(i)], w.at[feature_part(i)], w_sem.at[i]
        )

    for s in range(S):
        own_copy(s).start()
    for i in range(parts):
        w_copy(i).start()

    barrier = pltpu.get_barrier_semaphore()

    def greet(example, core):
        pl.semaphore_signal(
            barrier, inc=1, device_id={"example": example, "cls": core}, device_id_type=MESH
        )

    greet(me, sib)
    if Y == 2:
        greet(z * Y + (1 - y), k)

    @pl.when(z < Z - 1)
    def _():
        greet(me + Y, k)

    @pl.when(z > 0)
    def _():
        greet(me - Y, k)

    pl.semaphore_wait(barrier, Y + (z < Z - 1).astype(jnp.int32) + (z > 0).astype(jnp.int32))

    def forward(direction, s, slot, src):
        target = {
            INWARD: me + inward * Y,
            OUTWARD: me - inward * Y,
            SIDE: z * Y + (Y - 1 - y),
        }[direction]
        return remote(
            src, x.at[k, piece_rows(s, slot)], gsend.at[direction, s, slot],
            grecv.at[s, slot], target, k,
        )

    def to_sibling(s, slot, src):
        return remote(
            src, x.at[k, piece_rows(s, slot)], sib_send.at[s], sib_recv.at[s], me, sib
        )

    def arrived(s, slot):
        place = x.at[k, piece_rows(s, slot)]
        remote(place, place, gsend.at[SIDE, s, slot], grecv.at[s, slot], me, sib).wait_recv()

    def has_outer():
        return jnp.logical_and(z - inward >= 0, z - inward < Z)

    def own_sends(s, act):
        src = own_piece(s)
        act(forward(INWARD, s, me, src))

        @pl.when(has_outer())
        def _():
            act(forward(OUTWARD, s, me, src))

        if Y == 2:
            act(forward(SIDE, s, me, src))

    def begin(copy):
        copy.start()

    def finish(copy):
        copy.wait_send()

    def event(p, i, receive, act):
        end, mid = AT_END[i], AT_MID[i]
        s = p - jnp.where(is_end, AT_END_LAG[i], AT_MID_LAG[i])
        zz = z + inward * jnp.where(is_end, END_OFFSET[end], MID_OFFSET[mid])
        across = jnp.where(is_end, int(end in "DEFG"), int(mid in "DEFG"))
        slot = zz * Y + jnp.where(across == 1, 1 - y, y)
        odd = lax.rem(s, 2) == 1

        def any_of(*terms):
            out = None
            for use, condition in terms:
                if use:
                    out = condition if out is None else jnp.logical_or(out, condition)
            return out

        side = any_of(
            (end in "AB", is_end),
            (end == "C", jnp.logical_and(is_end, jnp.logical_not(odd))),
            (mid in "BC", is_mid),
        )
        inner = any_of((end == "D", is_end), (mid == "A", is_mid))
        outer = any_of((mid in "BC", is_mid), (mid == "G", jnp.logical_and(is_mid, odd)))

        @pl.when(jnp.logical_and(s >= 0, s < S))
        def _():
            src = x.at[k, piece_rows(s, slot)]
            if receive:
                arrived(s, slot)
            for condition, direction in ((outer, OUTWARD), (side, SIDE), (inner, INWARD)):
                if condition is not None:
                    @pl.when(condition)
                    def _():
                        act(forward(direction, s, slot, src))
            if receive:
                to_sibling(s, slot, src).start()

    def line(s, receive, act):
        def go(j, c):
            for sign in (-1, 1):
                zz = z + sign * j

                @pl.when(jnp.logical_and(zz >= 0, zz < Z))
                def _():
                    src = x.at[k, piece_rows(s, zz)]
                    if receive:
                        arrived(s, zz)
                    toward = jnp.where(inward == -sign, INWARD, OUTWARD)
                    target = z - sign

                    @pl.when(jnp.logical_and(target >= 0, target < Z))
                    def _():
                        act(remote(
                            src, src, gsend.at[toward, s, zz], grecv.at[s, zz], target, k
                        ))
                    if receive:
                        to_sibling(s, zz, src).start()
            return c

        lax.fori_loop(1, Z, go, 0)

    if Y == 2:
        assert Z == 4
        late = max(AT_END_LAG + AT_MID_LAG)
    else:
        late = 0
    ahead = min(AHEAD, S)

    for s in range(ahead):
        own_sends(s, begin)
    for s in range(S):
        to_sibling(s, me, own_piece(s)).start()

    def low_first(i):
        return remote(
            low_out.at[feature_part(i)], wlow.at[k, feature_part(i)],
            wsend.at[i], wrecv.at[i], me, sib,
        )

    def lower(i, c):
        part = feature_part(i)
        w_copy(i).wait()
        low_out[part, :] = w[part, columns(sib)].astype(BF16)
        low_first(i).start()
        wlow[k, part, :] = w[part, columns(k)].astype(BF16)
        return c

    def meta_copy(p):
        peer = lax.rem(me + p, n)
        return remote(meta_all.at[me], meta_all.at[me], msend, mrecv, peer, k)

    count = counts[0].astype(F32)
    label = labels[...]
    target_row = jnp.where(label >= active[0], label - active[0], label).astype(F32)
    meta_row = lax.broadcasted_iota(jnp.int32, (8, rows_n), 0)
    meta_all[me] = jnp.where(meta_row == 0, jnp.broadcast_to(target_row, (8, rows_n)), count)
    fsum[...] = jnp.zeros_like(fsum)

    active_count = active[0]
    class_base = mine * ck
    lane = lax.broadcasted_iota(jnp.int32, (LANES, LANES), 1)
    lane_float = lane.astype(F32)
    row_number = lax.broadcasted_iota(jnp.int32, (LANES, LANES), 0).astype(F32)

    def spread(row):
        return jnp.broadcast_to(row, (LANES, LANES)).T

    def share(piece, ssem, rsem, everyone):
        def copy(p):
            peer = lax.rem(mine + p, nd)
            return remote(piece, piece, ssem, rsem, peer // 2, lax.rem(peer, 2))

        def start():
            def go(p, c):
                copy(p).start()
                return c

            lax.fori_loop(1, nd, go, 0)

        def wait_in():
            remote(everyone, everyone, ssem, rsem, me, sib).wait_recv()

        def wait_out():
            remote(everyone, everyone, ssem, rsem, me, sib).wait_send()

        return start, wait_in, wait_out

    def share1(s):
        return share(
            stat1.at[s, mine], s1send.at[s], s1recv.at[s], stat1.at[s, pl.ds(0, nd - 1)]
        )

    def share2(b):
        return share(
            stat2.at[b, mine], s2send.at[b], s2recv.at[b], stat2.at[b, pl.ds(0, nd - 1)]
        )

    def exponents(base, rows, logits, with_label):
        index = class_base + lax.broadcasted_iota(jnp.int32, (rows, ck), 1)
        masked = jnp.where(index < active_count, logits, NEGATIVE)
        peak = jnp.max(masked, axis=1, keepdims=True)
        exponent = jnp.exp(masked - peak)
        total = jnp.sum(exponent, axis=1, keepdims=True)
        place = slice(base, base + rows) if isinstance(base, int) else pl.ds(pl.multiple_of(base, rows), rows)
        e_scr[place, :] = exponent
        if with_label:
            target = target_col[place, 0:1]
            label = jnp.sum(
                jnp.where(index.astype(F32) == target, logits, 0.0), axis=1, keepdims=True
            )
        count_rows = rows // LANES
        tile = jnp.zeros((LANES, LANES), F32)
        for j in range(count_rows):
            part = slice(j * LANES, (j + 1) * LANES)
            tile = jnp.where(lane == j, peak[part], tile)
            tile = jnp.where(lane == count_rows + j, total[part], tile)
            if with_label:
                tile = jnp.where(lane == 2 * count_rows + j, label[part], tile)
        return tile.T

    def combine(stat, b):
        count_rows = stat.shape[2] // 2
        tops, sums = slice(0, count_rows), slice(count_rows, 2 * count_rows)
        peak = stat[b, 0, tops]
        for d in range(1, nd):
            peak = jnp.maximum(peak, stat[b, d, tops])
        total = jnp.zeros_like(peak)
        for d in range(nd):
            total = total + stat[b, d, sums] * jnp.exp(stat[b, d, tops] - peak)
        return peak, total, jnp.exp(stat[b, mine, tops] - peak) / total

    def residuals(base, rows, factor, first):
        for j in range(rows // LANES):
            place = pl.ds(pl.multiple_of(base + j * LANES, LANES), LANES)
            weight = spread(factor[j:j + 1])
            valid = valid_col[place, :]
            target = target_col[place, :]
            if first:
                square = ssq[place, :]
            for c in range(ck // LANES):
                cols = slice(c * LANES, (c + 1) * LANES)
                probability = e_scr[place, cols] * weight
                index = lane_float + (class_base + c * LANES).astype(F32)
                is_label = (index == target).astype(F32)
                r_scr[k, place, cols] = (valid * (probability - is_label)).astype(BF16)
                if first:
                    fw = (valid * probability * (1.0 - probability)).astype(BF16)
                    fw_scr[k, place, cols] = fw
                    fsum[...] += fw.astype(F32) * square

    def swap(buffer, base, rows, ssem, rsem, owner):
        place = buffer.at[owner, pl.ds(pl.multiple_of(base, rows), rows)]
        return remote(place, place, ssem, rsem, me, sib)

    def clear(i, c):
        part = feature_part(i)
        moved[part, :] = jnp.zeros((step, 2 * ck), F32)
        for h in range(2):
            inv[h, part, :] = jnp.zeros((step, ck), F32)
        return c

    def task_logits(s):
        rows = round_rows(s)
        everything = x.at[sib, rows]
        own_copy(s).wait()
        remote(everything, everything, sib_send.at[s], sib_recv.at[s], me, sib).wait_recv()

        @pl.when(s == 0)
        def _():
            def arrive(i, c):
                part = wlow.at[sib, feature_part(i)]
                remote(part, part, wsend.at[i], wrecv.at[i], me, sib).wait_recv()
                low_first(i).wait_send()
                return c

            lax.fori_loop(0, parts, arrive, 0)

            def meta_start(p, c):
                meta_copy(p).start()
                return c

            lax.fori_loop(1, n, meta_start, 0)

        logits = jnp.dot(x[0, rows, :], wlow[0], preferred_element_type=F32)
        logits = logits + jnp.dot(x[1, rows, :], wlow[1], preferred_element_type=F32)
        tile = exponents(s * per_round, per_round, logits, False)
        stat1[s, mine] = tile[0:2 * groups, :]
        share1(s)[0]()
        squares = jnp.zeros((per_round, 1), F32)
        for h in range(2):
            block = x[h, rows, :]
            squares = squares + jnp.sum((block * block).astype(F32), axis=1, keepdims=True)
        ssq[rows, :] = jnp.broadcast_to(squares, (per_round, LANES))
        xt[:, rows] = x[k, rows, :].T

    start_d, in_d, out_d = share(
        damp_all.at[mine], dsend.at[0], drecv.at[0], damp_all.at[pl.ds(0, nd - 1)]
    )

    def task_residual(s):
        @pl.when(s == 0)
        def _():
            remote(
                meta_all.at[pl.ds(0, n - 1)], meta_all.at[pl.ds(0, n - 1)],
                msend, mrecv, me, sib,
            ).wait_recv()
            valid_total = meta_all[0, 1:2, :]
            for d in range(1, n):
                valid_total = valid_total + meta_all[d, 1:2, :]

            def spell(slot, c):
                target = spread(meta_all[slot, 0:1, :])
                valid = (row_number < meta_all[slot, 1:2, :]).astype(F32) / valid_total
                for t in range(S):
                    place = piece_rows(t, slot)
                    target_col[place, :] = target[t * q:(t + 1) * q]
                    valid_col[place, :] = valid[t * q:(t + 1) * q]
                return c

            lax.fori_loop(0, n, spell, 0)

        share1(s)[1]()
        factor = combine(stat1, s)[2]
        base = s * per_round
        residuals(base, per_round, factor, True)
        swap(r_scr, base, per_round, rsend.at[s], rrecv.at[s], k).start()
        swap(fw_scr, base, per_round, fsend.at[s], frecv.at[s], k).start()

        @pl.when(s == S - 1)
        def _():
            part = jnp.sum(jnp.sum(fsum[...], axis=0, keepdims=True), axis=1, keepdims=True)
            damp_all[mine] = jnp.broadcast_to(part, damp_all.shape[1:])
            start_d()

    def task_gradient(s, c):
        rows = round_rows(s)

        def go(i, carry):
            part = feature_part(i)
            block = xt[part, rows]
            moved[part, columns(c)] += jnp.dot(
                block, r_scr[c, rows, :], preferred_element_type=F32
            )
            inv[c, part, :] += jnp.dot(
                block * block, fw_scr[c, rows, :], preferred_element_type=F32
            )
            return carry

        lax.fori_loop(0, parts, go, 0, unroll=4)

    def when_round(s, act):
        @pl.when(jnp.logical_and(s >= 0, s < S))
        def _():
            act(s)

    def tasks(p, at):
        r = p - late - 1
        if at == TASK_L:
            when_round(r, task_logits)
        if at == TASK_R:
            when_round(r - 1, task_residual)
        if at == TASK_OWN:
            when_round(r - 1, lambda s: task_gradient(s, k))

            @pl.when(p == 0)
            def _():
                lax.fori_loop(0, parts, clear, 0)
        if at == TASK_SIB:
            def other(s):
                base = s * per_round
                swap(r_scr, base, per_round, rsend.at[s], rrecv.at[s], sib).wait_recv()
                swap(fw_scr, base, per_round, fsend.at[s], frecv.at[s], sib).wait_recv()
                task_gradient(s, sib)

            when_round(r - 1, other)

    lax.fori_loop(0, parts, lower, 0)

    def period(p, c):
        for i in range(7):
            if i == OWN_AT:
                when_round(p + ahead, lambda s: own_sends(s, begin))
            if Y == 2:
                event(p, i, True, begin)
            elif i == 0:
                when_round(p, lambda s: line(s, True, begin))
            tasks(p, i)
        return c

    lax.fori_loop(0, S + late + 2, period, 0)

    in_d()
    fisher_sum = damp_all[0, 0:1, 0:1]
    for d in range(1, nd):
        fisher_sum = fisher_sum + damp_all[d, 0:1, 0:1]
    damping = DAMPING_SHARE * fisher_sum / scale + EPSILON

    def update(i, c):
        part = feature_part(i)
        inverse = 1.0 / (inv[c, part, :] + damping)
        inv[c, part, :] = inverse
        change = moved[part, columns(c)] * inverse
        moved[part, columns(c)] = change
        return (w[part, columns(c)] - LEARNING_RATE * change).astype(BF16)

    def low_second(i):
        return remote(
            low_out.at[feature_part(i)], wlow.at[k, feature_part(i)],
            lsend.at[i], lrecv.at[i], me, sib,
        )

    def update_both(i):
        part = feature_part(i)
        low_out[part, :] = update(i, sib)
        low_second(i).start()
        low = update(i, k)
        term = jnp.dot(x[k, :, part], low, preferred_element_type=F32)
        if i == 0:
            e_scr[...] = term
        else:
            e_scr[...] += term

    for i in range(parts):
        update_both(i)

    def low_arrive(i, c):
        part = wlow.at[sib, feature_part(i)]
        remote(part, part, lsend.at[i], lrecv.at[i], me, sib).wait_recv()
        return c

    lax.fori_loop(0, parts, low_arrive, 0)

    def rounds_out(s, c):
        swap(r_scr, s * per_round, per_round, rsend.at[s], rrecv.at[s], k).wait_send()
        swap(fw_scr, s * per_round, per_round, fsend.at[s], frecv.at[s], k).wait_send()
        return c

    lax.fori_loop(0, S, rounds_out, 0)

    def second(b, c):
        rows = pl.ds(pl.multiple_of(b * HALF_ROWS, HALF_ROWS), HALF_ROWS)
        logits = e_scr[rows, :] + jnp.dot(
            x[sib, rows, :], wlow[sib], preferred_element_type=F32
        )
        tile = exponents(b * HALF_ROWS, HALF_ROWS, logits, True)
        stat2[b, mine] = tile[0:2 * per_half, :]
        labels_all[mine, pl.ds(b * per_half, per_half), :] = tile[2 * per_half:3 * per_half, :]
        share2(b)[0]()
        return c

    lax.fori_loop(0, halves, second, 0)

    start_l, in_l, out_l = share(
        labels_all.at[mine], dsend.at[1], drecv.at[1], labels_all.at[pl.ds(0, nd - 1)]
    )
    start_l()

    def swap2(b, owner):
        return swap(r_scr, b * HALF_ROWS, HALF_ROWS, r2send.at[b], r2recv.at[b], owner)

    def last(b, c):
        rows = pl.ds(pl.multiple_of(b * HALF_ROWS, HALF_ROWS), HALF_ROWS)
        sign = jnp.where(b == 0, -1.0, 1.0).astype(F32)
        share2(b)[1]()
        peak, total, factor = combine(stat2, b)
        residuals(b * HALF_ROWS, HALF_ROWS, factor, False)
        swap2(b, k).start()
        loss_row[b] = peak + jnp.log(total)

        def gradient(owner):
            def go(i, carry):
                part = feature_part(i)
                grad = jnp.dot(xt[part, rows], r_scr[owner, rows, :], preferred_element_type=F32)
                moved[part, columns(owner)] = (
                    sign * moved[part, columns(owner)] - grad * inv[owner, part, :]
                )
                return carry

            lax.fori_loop(0, parts, go, 0, unroll=4)

        gradient(k)
        swap2(b, sib).wait_recv()
        gradient(sib)
        return c

    lax.fori_loop(0, halves, last, 0)

    in_l()

    for b in range(halves):
        names = slice(b * per_half, (b + 1) * per_half)
        label = labels_all[0, names, :]
        for d in range(1, nd):
            label = label + labels_all[d, names, :]
        loss = loss_row[b] - label
        for j in range(per_half):
            at = b * HALF_ROWS + j * LANES
            loss_col[at:at + LANES, :] = spread(loss[j:j + 1])
    own = jnp.concatenate([loss_col[piece_rows(s, me), :] for s in range(S)], axis=0).T
    losses[...] = (lane_float[0:1] < count).astype(F32) * own[0:1, :]

    def drain(p, c):
        when_round(p, lambda s: own_sends(s, finish))
        if Y == 2:
            for i in range(7):
                event(p, i, False, finish)
        else:
            when_round(p, lambda s: line(s, False, finish))

        def rest(s):
            everything = x.at[k, round_rows(s)]
            remote(
                everything, everything, sib_send.at[s], sib_recv.at[s], me, sib
            ).wait_send()
            share1(s)[2]()

        when_round(p, rest)
        return c

    lax.fori_loop(0, S + late, drain, 0)
    remote(
        meta_all.at[pl.ds(0, n - 1)], meta_all.at[pl.ds(0, n - 1)], msend, mrecv, me, sib
    ).wait_send()
    out_d()
    out_l()

    def parts_out(i, c):
        low_second(i).wait_send()
        return c

    lax.fori_loop(0, parts, parts_out, 0)

    def halves_out(b, c):
        share2(b)[2]()
        swap2(b, k).wait_send()
        return c

    lax.fori_loop(0, halves, halves_out, 0)


def solution(mesh):
    n = mesh.shape["example"]
    Y = 2 if n == 8 else 1
    Z = n // Y
    nd = 2 * n

    def body(features, weights, labels, counts, active):
        rows_n, half = features.shape
        local = weights.shape[1]
        ck = local // 2
        all_rows = rows_n * n
        halves = all_rows // HALF_ROWS
        scale = float(half * 2 * local * n)
        parts = half // min(512, half)
        dma = pltpu.SemaphoreType.DMA
        moved, losses = pl.pallas_call(
            functools.partial(kernel, Z, Y, scale),
            out_shape=(
                pltpu.VMEM(weights.shape, F32),
                jax.ShapeDtypeStruct((1, rows_n), F32),
            ),
            in_specs=[
                pl.BlockSpec(memory_space=pl.ANY),
                pl.BlockSpec(memory_space=pl.ANY),
                pl.BlockSpec(memory_space=pltpu.VMEM),
                pl.BlockSpec(memory_space=pltpu.SMEM),
                pl.BlockSpec(memory_space=pltpu.SMEM),
            ],
            out_specs=(
                pl.BlockSpec(memory_space=pltpu.VMEM),
                pl.BlockSpec(memory_space=pltpu.VMEM),
            ),
            scratch_shapes=[
                pltpu.VMEM((2, all_rows, half), BF16),
                pltpu.VMEM((half, all_rows), BF16),
                pltpu.VMEM((half, local), F32),
                pltpu.VMEM((2, half, ck), BF16),
                pltpu.VMEM((half, ck), BF16),
                pltpu.VMEM((all_rows, ck), F32),
                pltpu.VMEM((2, all_rows, ck), BF16),
                pltpu.VMEM((2, all_rows, ck), BF16),
                pltpu.VMEM((2, half, ck), F32),
                pltpu.VMEM((n, 8, rows_n), F32),
                pltpu.VMEM((all_rows, LANES), F32),
                pltpu.VMEM((all_rows, LANES), F32),
                pltpu.VMEM((all_rows, LANES), F32),
                pltpu.VMEM((LANES, LANES), F32),
                pltpu.VMEM((ROUNDS, nd, 2 * (all_rows // ROUNDS // LANES), LANES), F32),
                pltpu.VMEM((halves, nd, 2 * (HALF_ROWS // LANES), LANES), F32),
                pltpu.VMEM((nd, 1, LANES), F32),
                pltpu.VMEM((nd, all_rows // LANES, LANES), F32),
                pltpu.VMEM((halves, HALF_ROWS // LANES, LANES), F32),
                pltpu.VMEM((all_rows, LANES), F32),
                dma((ROUNDS,)), dma((parts,)),
                dma((3, ROUNDS, n)), dma((ROUNDS, n)),
                dma((ROUNDS,)), dma((ROUNDS,)),
                dma((parts,)), dma((parts,)), dma((parts,)), dma((parts,)),
                dma, dma,
                dma((ROUNDS,)), dma((ROUNDS,)), dma((halves,)), dma((halves,)), dma((2,)), dma((2,)),
                dma((ROUNDS,)), dma((ROUNDS,)), dma((ROUNDS,)), dma((ROUNDS,)),
                dma((halves,)), dma((halves,)),
            ],
            compiler_params=pltpu.CompilerParams(
                collective_id=0, has_side_effects=True, vmem_limit_bytes=57671680
            ),
        )(features, weights, labels.reshape(1, rows_n), counts, active)
        return moved, losses.reshape(rows_n)

    return jax.shard_map(
        body,
        mesh=mesh,
        in_specs=(
            P(("groups", "example"), "cls"),
            P(("groups", "cls"), "example"),
            P(("groups", "example")),
            P(("groups", "example")),
            P("groups"),
        ),
        out_specs=(P(("groups", "cls"), "example"), P(("groups", "example"))),
        check_vma=False,
    )
```

```python
import functools

import jax
import jax.numpy as jnp
from jax import lax
from jax.experimental import pallas as pl
from jax.experimental.pallas import tpu as pltpu
from jax.sharding import PartitionSpec as P

NEGATIVE = -1e30
LEARNING_RATE = 2e-05
DAMPING_SHARE = 0.1
EPSILON = 1e-06
MESH = pl.DeviceIdType.MESH
INWARD, OUTWARD, SIDE = 0, 1, 2
F32, BF16 = jnp.float32, jnp.bfloat16

ROUNDS = 4
LANES = 128
HALF_ROWS = 512
AHEAD = 3
OWN_AT = 2
AT_END = "DCEAFBG"
AT_END_LAG = (0, 1, 1, 0, 1, 0, 1)
AT_MID = "ABEGDFC"
AT_MID_LAG = (0, 0, 1, 1, 0, 1, 0)
END_OFFSET = dict(A=1, B=2, C=3, D=0, E=1, F=2, G=3)
MID_OFFSET = dict(A=-1, B=1, C=2, D=0, E=1, F=-1, G=2)
TASK_L, TASK_R, TASK_OWN, TASK_SIB = 0, 4, 5, 6


def kernel(
    Z, Y, scale,
    features, weights, labels, counts, active,
    moved, losses,
    x, xt, w, wlow, low_out, e_scr, r_scr, fw_scr, inv,
    meta_all, target_col, valid_col, ssq, fsum, stat1, stat2, damp_all, labels_all, loss_row, loss_col,
    own_sem, w_sem, gsend, grecv, sib_send, sib_recv,
    wsend, wrecv, lsend, lrecv, msend, mrecv,
    s1send, s1recv, s2send, s2recv, dsend, drecv,
    rsend, rrecv, fsend, frecv, r2send, r2recv,
):
    n = Z * Y
    nd = 2 * n
    rows_n, half = features.shape
    S = ROUNDS
    q = rows_n // S
    per_round = n * q
    groups = per_round // LANES
    all_rows = n * rows_n
    ck = moved.shape[1] // 2
    step = min(512, half)
    parts = half // step
    halves = all_rows // HALF_ROWS
    per_half = HALF_ROWS // LANES
    me = lax.axis_index("example")
    k = lax.axis_index("cls")
    sib = 1 - k
    z, y = me // Y, lax.rem(me, Y)
    mine = me * 2 + k
    inward = jnp.where(z < Z // 2, 1, -1)
    is_end = jnp.logical_or(z == 0, z == Z - 1)
    is_mid = jnp.logical_not(is_end)

    def round_rows(s):
        return pl.ds(pl.multiple_of(s * per_round, per_round), per_round)

    def piece_rows(s, slot):
        return pl.ds(pl.multiple_of(s * per_round + slot * q, q), q)

    def columns(c):
        return pl.ds(pl.multiple_of(c * ck, ck), ck)

    def feature_part(i):
        return pl.ds(pl.multiple_of(i * step, step), step)

    def remote(src, dst, ssem, rsem, example, core):
        return pltpu.make_async_remote_copy(
            src_ref=src, dst_ref=dst, send_sem=ssem, recv_sem=rsem,
            device_id={"example": example, "cls": core}, device_id_type=MESH,
        )

    def own_piece(s):
        return features.at[pl.ds(pl.multiple_of(s * q, q), q)]

    def own_copy(s):
        return pltpu.make_async_copy(own_piece(s), x.at[k, piece_rows(s, me)], own_sem.at[s])

    def w_copy(i):
        return pltpu.make_async_copy(
            weights.at[feature_part(i)], w.at[feature_part(i)], w_sem.at[i]
        )

    for s in range(S):
        own_copy(s).start()
    for i in range(parts):
        w_copy(i).start()

    barrier = pltpu.get_barrier_semaphore()

    def greet(example, core):
        pl.semaphore_signal(
            barrier, inc=1, device_id={"example": example, "cls": core}, device_id_type=MESH
        )

    greet(me, sib)
    if Y == 2:
        greet(z * Y + (1 - y), k)

    @pl.when(z < Z - 1)
    def _():
        greet(me + Y, k)

    @pl.when(z > 0)
    def _():
        greet(me - Y, k)

    pl.semaphore_wait(barrier, Y + (z < Z - 1).astype(jnp.int32) + (z > 0).astype(jnp.int32))

    def forward(direction, s, slot, src):
        target = {
            INWARD: me + inward * Y,
            OUTWARD: me - inward * Y,
            SIDE: z * Y + (Y - 1 - y),
        }[direction]
        return remote(
            src, x.at[k, piece_rows(s, slot)], gsend.at[direction, s, slot],
            grecv.at[s, slot], target, k,
        )

    def to_sibling(s, slot, src):
        return remote(
            src, x.at[k, piece_rows(s, slot)], sib_send.at[s], sib_recv.at[s], me, sib
        )

    def arrived(s, slot):
        place = x.at[k, piece_rows(s, slot)]
        remote(place, place, gsend.at[SIDE, s, slot], grecv.at[s, slot], me, sib).wait_recv()

    def has_outer():
        return jnp.logical_and(z - inward >= 0, z - inward < Z)

    def own_sends(s, act):
        src = own_piece(s)
        act(forward(INWARD, s, me, src))

        @pl.when(has_outer())
        def _():
            act(forward(OUTWARD, s, me, src))

        if Y == 2:
            act(forward(SIDE, s, me, src))

    def begin(copy):
        copy.start()

    def finish(copy):
        copy.wait_send()

    def event(p, i, receive, act):
        end, mid = AT_END[i], AT_MID[i]
        s = p - jnp.where(is_end, AT_END_LAG[i], AT_MID_LAG[i])
        zz = z + inward * jnp.where(is_end, END_OFFSET[end], MID_OFFSET[mid])
        across = jnp.where(is_end, int(end in "DEFG"), int(mid in "DEFG"))
        slot = zz * Y + jnp.where(across == 1, 1 - y, y)
        odd = lax.rem(s, 2) == 1

        def any_of(*terms):
            out = None
            for use, condition in terms:
                if use:
                    out = condition if out is None else jnp.logical_or(out, condition)
            return out

        side = any_of(
            (end in "AB", is_end),
            (end == "C", jnp.logical_and(is_end, jnp.logical_not(odd))),
            (mid in "BC", is_mid),
        )
        inner = any_of((end == "D", is_end), (mid == "A", is_mid))
        outer = any_of((mid in "BC", is_mid), (mid == "G", jnp.logical_and(is_mid, odd)))

        @pl.when(jnp.logical_and(s >= 0, s < S))
        def _():
            src = x.at[k, piece_rows(s, slot)]
            if receive:
                arrived(s, slot)
            for condition, direction in ((outer, OUTWARD), (side, SIDE), (inner, INWARD)):
                if condition is not None:
                    @pl.when(condition)
                    def _():
                        act(forward(direction, s, slot, src))
            if receive:
                to_sibling(s, slot, src).start()

    def line(s, receive, act):
        def go(j, c):
            for sign in (-1, 1):
                zz = z + sign * j

                @pl.when(jnp.logical_and(zz >= 0, zz < Z))
                def _():
                    src = x.at[k, piece_rows(s, zz)]
                    if receive:
                        arrived(s, zz)
                    toward = jnp.where(inward == -sign, INWARD, OUTWARD)
                    target = z - sign

                    @pl.when(jnp.logical_and(target >= 0, target < Z))
                    def _():
                        act(remote(
                            src, src, gsend.at[toward, s, zz], grecv.at[s, zz], target, k
                        ))
                    if receive:
                        to_sibling(s, zz, src).start()
            return c

        lax.fori_loop(1, Z, go, 0)

    if Y == 2:
        assert Z == 4
        late = max(AT_END_LAG + AT_MID_LAG)
    else:
        late = 0
    ahead = min(AHEAD, S)

    for s in range(ahead):
        own_sends(s, begin)
    for s in range(S):
        to_sibling(s, me, own_piece(s)).start()

    def low_first(i):
        return remote(
            low_out.at[feature_part(i)], wlow.at[k, feature_part(i)],
            wsend.at[i], wrecv.at[i], me, sib,
        )

    def lower(i, c):
        part = feature_part(i)
        w_copy(i).wait()
        low_out[part, :] = w[part, columns(sib)].astype(BF16)
        low_first(i).start()
        wlow[k, part, :] = w[part, columns(k)].astype(BF16)
        return c

    def meta_copy(p):
        peer = lax.rem(me + p, n)
        return remote(meta_all.at[me], meta_all.at[me], msend, mrecv, peer, k)

    count = counts[0].astype(F32)
    label = labels[...]
    target_row = jnp.where(label >= active[0], label - active[0], label).astype(F32)
    meta_row = lax.broadcasted_iota(jnp.int32, (8, rows_n), 0)
    meta_all[me] = jnp.where(meta_row == 0, jnp.broadcast_to(target_row, (8, rows_n)), count)
    fsum[...] = jnp.zeros_like(fsum)

    active_count = active[0]
    class_base = mine * ck
    lane = lax.broadcasted_iota(jnp.int32, (LANES, LANES), 1)
    lane_float = lane.astype(F32)
    row_number = lax.broadcasted_iota(jnp.int32, (LANES, LANES), 0).astype(F32)

    def spread(row):
        return jnp.broadcast_to(row, (LANES, LANES)).T

    def share(piece, ssem, rsem, everyone):
        def copy(p):
            peer = lax.rem(mine + p, nd)
            return remote(piece, piece, ssem, rsem, peer // 2, lax.rem(peer, 2))

        def start():
            def go(p, c):
                copy(p).start()
                return c

            lax.fori_loop(1, nd, go, 0)

        def wait_in():
            remote(everyone, everyone, ssem, rsem, me, sib).wait_recv()

        def wait_out():
            remote(everyone, everyone, ssem, rsem, me, sib).wait_send()

        return start, wait_in, wait_out

    def share1(s):
        return share(
            stat1.at[s, mine], s1send.at[s], s1recv.at[s], stat1.at[s, pl.ds(0, nd - 1)]
        )

    def share2(b):
        return share(
            stat2.at[b, mine], s2send.at[b], s2recv.at[b], stat2.at[b, pl.ds(0, nd - 1)]
        )

    def exponents(base, rows, logits, with_label):
        index = class_base + lax.broadcasted_iota(jnp.int32, (rows, ck), 1)
        masked = jnp.where(index < active_count, logits, NEGATIVE)
        peak = jnp.max(masked, axis=1, keepdims=True)
        exponent = jnp.exp(masked - peak)
        total = jnp.sum(exponent, axis=1, keepdims=True)
        place = slice(base, base + rows) if isinstance(base, int) else pl.ds(pl.multiple_of(base, rows), rows)
        e_scr[place, :] = exponent
        if with_label:
            target = target_col[place, 0:1]
            label = jnp.sum(
                jnp.where(index.astype(F32) == target, logits, 0.0), axis=1, keepdims=True
            )
        count_rows = rows // LANES
        tile = jnp.zeros((LANES, LANES), F32)
        for j in range(count_rows):
            part = slice(j * LANES, (j + 1) * LANES)
            tile = jnp.where(lane == j, peak[part], tile)
            tile = jnp.where(lane == count_rows + j, total[part], tile)
            if with_label:
                tile = jnp.where(lane == 2 * count_rows + j, label[part], tile)
        return tile.T

    def combine(stat, b):
        count_rows = stat.shape[2] // 2
        tops, sums = slice(0, count_rows), slice(count_rows, 2 * count_rows)
        peak = stat[b, 0, tops]
        for d in range(1, nd):
            peak = jnp.maximum(peak, stat[b, d, tops])
        total = jnp.zeros_like(peak)
        for d in range(nd):
            total = total + stat[b, d, sums] * jnp.exp(stat[b, d, tops] - peak)
        return peak, total, jnp.exp(stat[b, mine, tops] - peak) / total

    def residuals(base, rows, factor, first):
        for j in range(rows // LANES):
            place = pl.ds(pl.multiple_of(base + j * LANES, LANES), LANES)
            weight = spread(factor[j:j + 1])
            valid = valid_col[place, :]
            target = target_col[place, :]
            if first:
                square = ssq[place, :]
            for c in range(ck // LANES):
                cols = slice(c * LANES, (c + 1) * LANES)
                probability = e_scr[place, cols] * weight
                index = lane_float + (class_base + c * LANES).astype(F32)
                is_label = (index == target).astype(F32)
                r_scr[k, place, cols] = (valid * (probability - is_label)).astype(BF16)
                if first:
                    fw = (valid * probability * (1.0 - probability)).astype(BF16)
                    fw_scr[k, place, cols] = fw
                    fsum[...] += fw.astype(F32) * square

    def swap(buffer, base, rows, ssem, rsem, owner):
        place = buffer.at[owner, pl.ds(pl.multiple_of(base, rows), rows)]
        return remote(place, place, ssem, rsem, me, sib)

    def clear(i, c):
        part = feature_part(i)
        moved[part, :] = jnp.zeros((step, 2 * ck), F32)
        for h in range(2):
            inv[h, part, :] = jnp.zeros((step, ck), F32)
        return c

    def task_logits(s):
        rows = round_rows(s)
        everything = x.at[sib, rows]
        own_copy(s).wait()
        remote(everything, everything, sib_send.at[s], sib_recv.at[s], me, sib).wait_recv()

        @pl.when(s == 0)
        def _():
            def arrive(i, c):
                part = wlow.at[sib, feature_part(i)]
                remote(part, part, wsend.at[i], wrecv.at[i], me, sib).wait_recv()
                low_first(i).wait_send()
                return c

            lax.fori_loop(0, parts, arrive, 0)

            def meta_start(p, c):
                meta_copy(p).start()
                return c

            lax.fori_loop(1, n, meta_start, 0)

        logits = jnp.dot(x[0, rows, :], wlow[0], preferred_element_type=F32)
        logits = logits + jnp.dot(x[1, rows, :], wlow[1], preferred_element_type=F32)
        tile = exponents(s * per_round, per_round, logits, False)
        stat1[s, mine] = tile[0:2 * groups, :]
        share1(s)[0]()
        squares = jnp.zeros((per_round, 1), F32)
        for h in range(2):
            block = x[h, rows, :]
            squares = squares + jnp.sum((block * block).astype(F32), axis=1, keepdims=True)
        ssq[rows, :] = jnp.broadcast_to(squares, (per_round, LANES))
        xt[:, rows] = x[k, rows, :].T

    start_d, in_d, out_d = share(
        damp_all.at[mine], dsend.at[0], drecv.at[0], damp_all.at[pl.ds(0, nd - 1)]
    )

    def task_residual(s):
        @pl.when(s == 0)
        def _():
            remote(
                meta_all.at[pl.ds(0, n - 1)], meta_all.at[pl.ds(0, n - 1)],
                msend, mrecv, me, sib,
            ).wait_recv()
            valid_total = meta_all[0, 1:2, :]
            for d in range(1, n):
                valid_total = valid_total + meta_all[d, 1:2, :]

            def spell(slot, c):
                target = spread(meta_all[slot, 0:1, :])
                valid = (row_number < meta_all[slot, 1:2, :]).astype(F32) / valid_total
                for t in range(S):
                    place = piece_rows(t, slot)
                    target_col[place, :] = target[t * q:(t + 1) * q]
                    valid_col[place, :] = valid[t * q:(t + 1) * q]
                return c

            lax.fori_loop(0, n, spell, 0)

        share1(s)[1]()
        factor = combine(stat1, s)[2]
        base = s * per_round
        residuals(base, per_round, factor, True)
        swap(r_scr, base, per_round, rsend.at[s], rrecv.at[s], k).start()
        swap(fw_scr, base, per_round, fsend.at[s], frecv.at[s], k).start()

        @pl.when(s == S - 1)
        def _():
            part = jnp.sum(jnp.sum(fsum[...], axis=0, keepdims=True), axis=1, keepdims=True)
            damp_all[mine] = jnp.broadcast_to(part, damp_all.shape[1:])
            start_d()

    def task_gradient(s, c):
        rows = round_rows(s)

        def go(i, carry):
            part = feature_part(i)
            block = xt[part, rows]
            moved[part, columns(c)] += jnp.dot(
                block, r_scr[c, rows, :], preferred_element_type=F32
            )
            inv[c, part, :] += jnp.dot(
                block * block, fw_scr[c, rows, :], preferred_element_type=F32
            )
            return carry

        lax.fori_loop(0, parts, go, 0, unroll=4)

    def when_round(s, act):
        @pl.when(jnp.logical_and(s >= 0, s < S))
        def _():
            act(s)

    def tasks(p, at):
        r = p - late - 1
        if at == TASK_L:
            when_round(r, task_logits)
        if at == TASK_R:
            when_round(r - 1, task_residual)
        if at == TASK_OWN:
            when_round(r - 1, lambda s: task_gradient(s, k))

            @pl.when(p == 0)
            def _():
                lax.fori_loop(0, parts, clear, 0)
        if at == TASK_SIB:
            def other(s):
                base = s * per_round
                swap(r_scr, base, per_round, rsend.at[s], rrecv.at[s], sib).wait_recv()
                swap(fw_scr, base, per_round, fsend.at[s], frecv.at[s], sib).wait_recv()
                task_gradient(s, sib)

            when_round(r - 1, other)

    lax.fori_loop(0, parts, lower, 0)

    def period(p, c):
        for i in range(7):
            if i == OWN_AT:
                when_round(p + ahead, lambda s: own_sends(s, begin))
            if Y == 2:
                event(p, i, True, begin)
            elif i == 0:
                when_round(p, lambda s: line(s, True, begin))
            tasks(p, i)
        return c

    lax.fori_loop(0, S + late + 2, period, 0)

    in_d()
    fisher_sum = damp_all[0, 0:1, 0:1]
    for d in range(1, nd):
        fisher_sum = fisher_sum + damp_all[d, 0:1, 0:1]
    damping = DAMPING_SHARE * fisher_sum / scale + EPSILON

    def update(i, c):
        part = feature_part(i)
        inverse = 1.0 / (inv[c, part, :] + damping)
        inv[c, part, :] = inverse
        change = moved[part, columns(c)] * inverse
        moved[part, columns(c)] = change
        return (w[part, columns(c)] - LEARNING_RATE * change).astype(BF16)

    def low_second(i):
        return remote(
            low_out.at[feature_part(i)], wlow.at[k, feature_part(i)],
            lsend.at[i], lrecv.at[i], me, sib,
        )

    def update_both(i):
        part = feature_part(i)
        low_out[part, :] = update(i, sib)
        low_second(i).start()
        low = update(i, k)
        term = jnp.dot(x[k, :, part], low, preferred_element_type=F32)
        if i == 0:
            e_scr[...] = term
        else:
            e_scr[...] += term

    for i in range(parts):
        update_both(i)

    def low_arrive(i, c):
        part = wlow.at[sib, feature_part(i)]
        remote(part, part, lsend.at[i], lrecv.at[i], me, sib).wait_recv()
        return c

    lax.fori_loop(0, parts, low_arrive, 0)

    def second(b, c):
        rows = pl.ds(pl.multiple_of(b * HALF_ROWS, HALF_ROWS), HALF_ROWS)
        logits = e_scr[rows, :] + jnp.dot(
            x[sib, rows, :], wlow[sib], preferred_element_type=F32
        )
        tile = exponents(b * HALF_ROWS, HALF_ROWS, logits, True)
        stat2[b, mine] = tile[0:2 * per_half, :]
        labels_all[mine, pl.ds(b * per_half, per_half), :] = tile[2 * per_half:3 * per_half, :]
        share2(b)[0]()
        return c

    lax.fori_loop(0, halves, second, 0)

    start_l, in_l, out_l = share(
        labels_all.at[mine], dsend.at[1], drecv.at[1], labels_all.at[pl.ds(0, nd - 1)]
    )
    start_l()

    def rounds_out(s, c):
        swap(r_scr, s * per_round, per_round, rsend.at[s], rrecv.at[s], k).wait_send()
        swap(fw_scr, s * per_round, per_round, fsend.at[s], frecv.at[s], k).wait_send()
        return c

    lax.fori_loop(0, S, rounds_out, 0)

    def drain(p, c):
        when_round(p, lambda s: own_sends(s, finish))
        if Y == 2:
            for i in range(7):
                event(p, i, False, finish)
        else:
            when_round(p, lambda s: line(s, False, finish))

        def rest(s):
            everything = x.at[k, round_rows(s)]
            remote(
                everything, everything, sib_send.at[s], sib_recv.at[s], me, sib
            ).wait_send()
            share1(s)[2]()

        when_round(p, rest)
        return c

    lax.fori_loop(0, S + late, drain, 0)
    remote(
        meta_all.at[pl.ds(0, n - 1)], meta_all.at[pl.ds(0, n - 1)], msend, mrecv, me, sib
    ).wait_send()
    out_d()

    def parts_out(i, c):
        low_second(i).wait_send()
        return c

    lax.fori_loop(0, parts, parts_out, 0)

    def swap2(b, owner):
        return swap(r_scr, b * HALF_ROWS, HALF_ROWS, r2send.at[b], r2recv.at[b], owner)

    def last(b, c):
        rows = pl.ds(pl.multiple_of(b * HALF_ROWS, HALF_ROWS), HALF_ROWS)
        sign = jnp.where(b == 0, -1.0, 1.0).astype(F32)
        share2(b)[1]()
        peak, total, factor = combine(stat2, b)
        residuals(b * HALF_ROWS, HALF_ROWS, factor, False)
        swap2(b, k).start()
        loss_row[b] = peak + jnp.log(total)

        def gradient(owner):
            def go(i, carry):
                part = feature_part(i)
                grad = jnp.dot(xt[part, rows], r_scr[owner, rows, :], preferred_element_type=F32)
                moved[part, columns(owner)] = (
                    sign * moved[part, columns(owner)] - grad * inv[owner, part, :]
                )
                return carry

            lax.fori_loop(0, parts, go, 0, unroll=4)

        gradient(k)
        swap2(b, sib).wait_recv()
        gradient(sib)
        return c

    lax.fori_loop(0, halves, last, 0)

    in_l()

    for b in range(halves):
        names = slice(b * per_half, (b + 1) * per_half)
        label = labels_all[0, names, :]
        for d in range(1, nd):
            label = label + labels_all[d, names, :]
        loss = loss_row[b] - label
        for j in range(per_half):
            at = b * HALF_ROWS + j * LANES
            loss_col[at:at + LANES, :] = spread(loss[j:j + 1])
    own = jnp.concatenate([loss_col[piece_rows(s, me), :] for s in range(S)], axis=0).T
    losses[...] = (lane_float[0:1] < count).astype(F32) * own[0:1, :]

    out_l()

    def halves_out(b, c):
        share2(b)[2]()
        swap2(b, k).wait_send()
        return c

    lax.fori_loop(0, halves, halves_out, 0)


def solution(mesh):
    n = mesh.shape["example"]
    Y = 2 if n == 8 else 1
    Z = n // Y
    nd = 2 * n

    def body(features, weights, labels, counts, active):
        rows_n, half = features.shape
        local = weights.shape[1]
        ck = local // 2
        all_rows = rows_n * n
        halves = all_rows // HALF_ROWS
        scale = float(half * 2 * local * n)
        parts = half // min(512, half)
        dma = pltpu.SemaphoreType.DMA
        moved, losses = pl.pallas_call(
            functools.partial(kernel, Z, Y, scale),
            out_shape=(
                pltpu.VMEM(weights.shape, F32),
                jax.ShapeDtypeStruct((1, rows_n), F32),
            ),
            in_specs=[
                pl.BlockSpec(memory_space=pl.ANY),
                pl.BlockSpec(memory_space=pl.ANY),
                pl.BlockSpec(memory_space=pltpu.VMEM),
                pl.BlockSpec(memory_space=pltpu.SMEM),
                pl.BlockSpec(memory_space=pltpu.SMEM),
            ],
            out_specs=(
                pl.BlockSpec(memory_space=pltpu.VMEM),
                pl.BlockSpec(memory_space=pltpu.VMEM),
            ),
            scratch_shapes=[
                pltpu.VMEM((2, all_rows, half), BF16),
                pltpu.VMEM((half, all_rows), BF16),
                pltpu.VMEM((half, local), F32),
                pltpu.VMEM((2, half, ck), BF16),
                pltpu.VMEM((half, ck), BF16),
                pltpu.VMEM((all_rows, ck), F32),
                pltpu.VMEM((2, all_rows, ck), BF16),
                pltpu.VMEM((2, all_rows, ck), BF16),
                pltpu.VMEM((2, half, ck), F32),
                pltpu.VMEM((n, 8, rows_n), F32),
                pltpu.VMEM((all_rows, LANES), F32),
                pltpu.VMEM((all_rows, LANES), F32),
                pltpu.VMEM((all_rows, LANES), F32),
                pltpu.VMEM((LANES, LANES), F32),
                pltpu.VMEM((ROUNDS, nd, 2 * (all_rows // ROUNDS // LANES), LANES), F32),
                pltpu.VMEM((halves, nd, 2 * (HALF_ROWS // LANES), LANES), F32),
                pltpu.VMEM((nd, 1, LANES), F32),
                pltpu.VMEM((nd, all_rows // LANES, LANES), F32),
                pltpu.VMEM((halves, HALF_ROWS // LANES, LANES), F32),
                pltpu.VMEM((all_rows, LANES), F32),
                dma((ROUNDS,)), dma((parts,)),
                dma((3, ROUNDS, n)), dma((ROUNDS, n)),
                dma((ROUNDS,)), dma((ROUNDS,)),
                dma((parts,)), dma((parts,)), dma((parts,)), dma((parts,)),
                dma, dma,
                dma((ROUNDS,)), dma((ROUNDS,)), dma((halves,)), dma((halves,)), dma((2,)), dma((2,)),
                dma((ROUNDS,)), dma((ROUNDS,)), dma((ROUNDS,)), dma((ROUNDS,)),
                dma((halves,)), dma((halves,)),
            ],
            compiler_params=pltpu.CompilerParams(
                collective_id=0, has_side_effects=True, vmem_limit_bytes=57671680
            ),
        )(features, weights, labels.reshape(1, rows_n), counts, active)
        return moved, losses.reshape(rows_n)

    return jax.shard_map(
        body,
        mesh=mesh,
        in_specs=(
            P(("groups", "example"), "cls"),
            P(("groups", "cls"), "example"),
            P(("groups", "example")),
            P(("groups", "example")),
            P("groups"),
        ),
        out_specs=(P(("groups", "cls"), "example"), P(("groups", "example"))),
        check_vma=False,
    )
```

```python
import functools

import jax
import jax.numpy as jnp
from jax import lax
from jax.experimental import pallas as pl
from jax.experimental.pallas import tpu as pltpu
from jax.sharding import PartitionSpec as P

NEGATIVE = -1e30
LEARNING_RATE = 2e-05
DAMPING_SHARE = 0.1
EPSILON = 1e-06
MESH = pl.DeviceIdType.MESH
INWARD, OUTWARD, SIDE = 0, 1, 2
F32, BF16 = jnp.float32, jnp.bfloat16

ROUNDS = 4
LANES = 128
HALF_ROWS = 512
AHEAD = 3
OWN_AT = 2
AT_END = "DCEAFBG"
AT_END_LAG = (0, 1, 1, 0, 1, 0, 1)
AT_MID = "ABEGDFC"
AT_MID_LAG = (0, 0, 1, 1, 0, 1, 0)
END_OFFSET = dict(A=1, B=2, C=3, D=0, E=1, F=2, G=3)
MID_OFFSET = dict(A=-1, B=1, C=2, D=0, E=1, F=-1, G=2)
TASK_L, TASK_R, TASK_OWN, TASK_SIB = 0, 4, 5, 6


def kernel(
    Z, Y, scale,
    features, weights, labels, counts, active,
    moved, losses,
    x, xt, w, wlow, low_out, e_scr, r_scr, fw_scr, inv,
    meta_all, target_col, valid_col, ssq, fsum, stat1, stat2, damp_all, labels_all, loss_row, loss_col,
    own_sem, w_sem, gsend, grecv, sib_send, sib_recv,
    wsend, wrecv, lsend, lrecv, msend, mrecv,
    s1send, s1recv, s2send, s2recv, dsend, drecv,
    rsend, rrecv, fsend, frecv, r2send, r2recv,
):
    n = Z * Y
    nd = 2 * n
    rows_n, half = features.shape
    S = ROUNDS
    q = rows_n // S
    per_round = n * q
    groups = per_round // LANES
    all_rows = n * rows_n
    ck = moved.shape[1] // 2
    step = min(512, half)
    parts = half // step
    halves = all_rows // HALF_ROWS
    per_half = HALF_ROWS // LANES
    me = lax.axis_index("example")
    k = lax.axis_index("cls")
    sib = 1 - k
    z, y = me // Y, lax.rem(me, Y)
    mine = me * 2 + k
    inward = jnp.where(z < Z // 2, 1, -1)
    is_end = jnp.logical_or(z == 0, z == Z - 1)
    is_mid = jnp.logical_not(is_end)

    def round_rows(s):
        return pl.ds(pl.multiple_of(s * per_round, per_round), per_round)

    def piece_rows(s, slot):
        return pl.ds(pl.multiple_of(s * per_round + slot * q, q), q)

    def columns(c):
        return pl.ds(pl.multiple_of(c * ck, ck), ck)

    def feature_part(i):
        return pl.ds(pl.multiple_of(i * step, step), step)

    def remote(src, dst, ssem, rsem, example, core):
        return pltpu.make_async_remote_copy(
            src_ref=src, dst_ref=dst, send_sem=ssem, recv_sem=rsem,
            device_id={"example": example, "cls": core}, device_id_type=MESH,
        )

    def own_piece(s):
        return features.at[pl.ds(pl.multiple_of(s * q, q), q)]

    def own_copy(s):
        return pltpu.make_async_copy(own_piece(s), x.at[k, piece_rows(s, me)], own_sem.at[s])

    def w_copy(i):
        return pltpu.make_async_copy(
            weights.at[feature_part(i)], w.at[feature_part(i)], w_sem.at[i]
        )

    for s in range(S):
        own_copy(s).start()
    for i in range(parts):
        w_copy(i).start()

    barrier = pltpu.get_barrier_semaphore()

    def greet(example, core):
        pl.semaphore_signal(
            barrier, inc=1, device_id={"example": example, "cls": core}, device_id_type=MESH
        )

    greet(me, sib)
    if Y == 2:
        greet(z * Y + (1 - y), k)

    @pl.when(z < Z - 1)
    def _():
        greet(me + Y, k)

    @pl.when(z > 0)
    def _():
        greet(me - Y, k)

    pl.semaphore_wait(barrier, Y + (z < Z - 1).astype(jnp.int32) + (z > 0).astype(jnp.int32))

    def forward(direction, s, slot, src):
        target = {
            INWARD: me + inward * Y,
            OUTWARD: me - inward * Y,
            SIDE: z * Y + (Y - 1 - y),
        }[direction]
        return remote(
            src, x.at[k, piece_rows(s, slot)], gsend.at[direction, s, slot],
            grecv.at[s, slot], target, k,
        )

    def to_sibling(s, slot, src):
        return remote(
            src, x.at[k, piece_rows(s, slot)], sib_send.at[s], sib_recv.at[s], me, sib
        )

    def arrived(s, slot):
        place = x.at[k, piece_rows(s, slot)]
        remote(place, place, gsend.at[SIDE, s, slot], grecv.at[s, slot], me, sib).wait_recv()

    def has_outer():
        return jnp.logical_and(z - inward >= 0, z - inward < Z)

    def own_sends(s, act):
        src = own_piece(s)
        act(forward(INWARD, s, me, src))

        @pl.when(has_outer())
        def _():
            act(forward(OUTWARD, s, me, src))

        if Y == 2:
            act(forward(SIDE, s, me, src))

    def begin(copy):
        copy.start()

    def finish(copy):
        copy.wait_send()

    def event(p, i, receive, act):
        end, mid = AT_END[i], AT_MID[i]
        s = p - jnp.where(is_end, AT_END_LAG[i], AT_MID_LAG[i])
        zz = z + inward * jnp.where(is_end, END_OFFSET[end], MID_OFFSET[mid])
        across = jnp.where(is_end, int(end in "DEFG"), int(mid in "DEFG"))
        slot = zz * Y + jnp.where(across == 1, 1 - y, y)
        odd = lax.rem(s, 2) == 1

        def any_of(*terms):
            out = None
            for use, condition in terms:
                if use:
                    out = condition if out is None else jnp.logical_or(out, condition)
            return out

        side = any_of(
            (end in "AB", is_end),
            (end == "C", jnp.logical_and(is_end, jnp.logical_not(odd))),
            (mid in "BC", is_mid),
        )
        inner = any_of((end == "D", is_end), (mid == "A", is_mid))
        outer = any_of((mid in "BC", is_mid), (mid == "G", jnp.logical_and(is_mid, odd)))

        @pl.when(jnp.logical_and(s >= 0, s < S))
        def _():
            src = x.at[k, piece_rows(s, slot)]
            if receive:
                arrived(s, slot)
            for condition, direction in ((outer, OUTWARD), (side, SIDE), (inner, INWARD)):
                if condition is not None:
                    @pl.when(condition)
                    def _():
                        act(forward(direction, s, slot, src))
            if receive:
                to_sibling(s, slot, src).start()

    def line(s, receive, act):
        def go(j, c):
            for sign in (-1, 1):
                zz = z + sign * j

                @pl.when(jnp.logical_and(zz >= 0, zz < Z))
                def _():
                    src = x.at[k, piece_rows(s, zz)]
                    if receive:
                        arrived(s, zz)
                    toward = jnp.where(inward == -sign, INWARD, OUTWARD)
                    target = z - sign

                    @pl.when(jnp.logical_and(target >= 0, target < Z))
                    def _():
                        act(remote(
                            src, src, gsend.at[toward, s, zz], grecv.at[s, zz], target, k
                        ))
                    if receive:
                        to_sibling(s, zz, src).start()
            return c

        lax.fori_loop(1, Z, go, 0)

    if Y == 2:
        assert Z == 4
        late = max(AT_END_LAG + AT_MID_LAG)
    else:
        late = 0
    ahead = min(AHEAD, S)

    for s in range(ahead):
        own_sends(s, begin)
    for s in range(S):
        to_sibling(s, me, own_piece(s)).start()

    def low_first(i):
        return remote(
            low_out.at[feature_part(i)], wlow.at[k, feature_part(i)],
            wsend.at[i], wrecv.at[i], me, sib,
        )

    def lower(i, c):
        part = feature_part(i)
        w_copy(i).wait()
        low_out[part, :] = w[part, columns(sib)].astype(BF16)
        low_first(i).start()
        wlow[k, part, :] = w[part, columns(k)].astype(BF16)
        return c

    def meta_copy(p):
        peer = lax.rem(me + p, n)
        return remote(meta_all.at[me], meta_all.at[me], msend, mrecv, peer, k)

    count = counts[0].astype(F32)
    label = labels[...]
    target_row = jnp.where(label >= active[0], label - active[0], label).astype(F32)
    meta_row = lax.broadcasted_iota(jnp.int32, (8, rows_n), 0)
    meta_all[me] = jnp.where(meta_row == 0, jnp.broadcast_to(target_row, (8, rows_n)), count)
    fsum[...] = jnp.zeros_like(fsum)

    active_count = active[0]
    class_base = mine * ck
    lane = lax.broadcasted_iota(jnp.int32, (LANES, LANES), 1)
    lane_float = lane.astype(F32)
    row_number = lax.broadcasted_iota(jnp.int32, (LANES, LANES), 0).astype(F32)

    def spread(row):
        return jnp.broadcast_to(row, (LANES, LANES)).T

    def share(piece, ssem, rsem, everyone):
        def copy(p):
            peer = lax.rem(mine + p, nd)
            return remote(piece, piece, ssem, rsem, peer // 2, lax.rem(peer, 2))

        def start():
            def go(p, c):
                copy(p).start()
                return c

            lax.fori_loop(1, nd, go, 0)

        def wait_in():
            remote(everyone, everyone, ssem, rsem, me, sib).wait_recv()

        def wait_out():
            remote(everyone, everyone, ssem, rsem, me, sib).wait_send()

        return start, wait_in, wait_out

    def share1(s):
        return share(
            stat1.at[s, mine], s1send.at[s], s1recv.at[s], stat1.at[s, pl.ds(0, nd - 1)]
        )

    def share2(b):
        return share(
            stat2.at[b, mine], s2send.at[b], s2recv.at[b], stat2.at[b, pl.ds(0, nd - 1)]
        )

    def exponents(base, rows, logits, with_label):
        index = class_base + lax.broadcasted_iota(jnp.int32, (rows, ck), 1)
        masked = jnp.where(index < active_count, logits, NEGATIVE)
        peak = jnp.max(masked, axis=1, keepdims=True)
        exponent = jnp.exp(masked - peak)
        total = jnp.sum(exponent, axis=1, keepdims=True)
        place = slice(base, base + rows) if isinstance(base, int) else pl.ds(pl.multiple_of(base, rows), rows)
        e_scr[place, :] = exponent
        if with_label:
            target = target_col[place, 0:1]
            label = jnp.sum(
                jnp.where(index.astype(F32) == target, logits, 0.0), axis=1, keepdims=True
            )
        count_rows = rows // LANES
        tile = jnp.zeros((LANES, LANES), F32)
        for j in range(count_rows):
            part = slice(j * LANES, (j + 1) * LANES)
            tile = jnp.where(lane == j, peak[part], tile)
            tile = jnp.where(lane == count_rows + j, total[part], tile)
            if with_label:
                tile = jnp.where(lane == 2 * count_rows + j, label[part], tile)
        return tile.T

    def combine(stat, b):
        count_rows = stat.shape[2] // 2
        tops, sums = slice(0, count_rows), slice(count_rows, 2 * count_rows)
        peak = stat[b, 0, tops]
        for d in range(1, nd):
            peak = jnp.maximum(peak, stat[b, d, tops])
        total = jnp.zeros_like(peak)
        for d in range(nd):
            total = total + stat[b, d, sums] * jnp.exp(stat[b, d, tops] - peak)
        return peak, total, jnp.exp(stat[b, mine, tops] - peak) / total

    def residuals(base, rows, factor, first):
        for j in range(rows // LANES):
            place = pl.ds(pl.multiple_of(base + j * LANES, LANES), LANES)
            weight = spread(factor[j:j + 1])
            valid = valid_col[place, :]
            target = target_col[place, :]
            if first:
                square = ssq[place, :]
            for c in range(ck // LANES):
                cols = slice(c * LANES, (c + 1) * LANES)
                probability = e_scr[place, cols] * weight
                index = lane_float + (class_base + c * LANES).astype(F32)
                is_label = (index == target).astype(F32)
                r_scr[k, place, cols] = (valid * (probability - is_label)).astype(BF16)
                if first:
                    fw = (valid * probability * (1.0 - probability)).astype(BF16)
                    fw_scr[k, place, cols] = fw
                    fsum[...] += fw.astype(F32) * square

    def swap(buffer, base, rows, ssem, rsem, owner):
        place = buffer.at[owner, pl.ds(pl.multiple_of(base, rows), rows)]
        return remote(place, place, ssem, rsem, me, sib)

    def clear(i, c):
        part = feature_part(i)
        moved[part, :] = jnp.zeros((step, 2 * ck), F32)
        for h in range(2):
            inv[h, part, :] = jnp.zeros((step, ck), F32)
        return c

    def task_logits(s):
        rows = round_rows(s)
        everything = x.at[sib, rows]
        own_copy(s).wait()
        remote(everything, everything, sib_send.at[s], sib_recv.at[s], me, sib).wait_recv()

        @pl.when(s == 0)
        def _():
            def arrive(i, c):
                part = wlow.at[sib, feature_part(i)]
                remote(part, part, wsend.at[i], wrecv.at[i], me, sib).wait_recv()
                low_first(i).wait_send()
                return c

            lax.fori_loop(0, parts, arrive, 0)

            def meta_start(p, c):
                meta_copy(p).start()
                return c

            lax.fori_loop(1, n, meta_start, 0)

        logits = jnp.dot(x[0, rows, :], wlow[0], preferred_element_type=F32)
        logits = logits + jnp.dot(x[1, rows, :], wlow[1], preferred_element_type=F32)
        tile = exponents(s * per_round, per_round, logits, False)
        stat1[s, mine] = tile[0:2 * groups, :]
        share1(s)[0]()
        squares = jnp.zeros((per_round, 1), F32)
        for h in range(2):
            block = x[h, rows, :]
            squares = squares + jnp.sum((block * block).astype(F32), axis=1, keepdims=True)
        ssq[rows, :] = jnp.broadcast_to(squares, (per_round, LANES))
        xt[:, rows] = x[k, rows, :].T

    start_d, in_d, out_d = share(
        damp_all.at[mine], dsend.at[0], drecv.at[0], damp_all.at[pl.ds(0, nd - 1)]
    )

    def task_residual(s):
        @pl.when(s == 0)
        def _():
            remote(
                meta_all.at[pl.ds(0, n - 1)], meta_all.at[pl.ds(0, n - 1)],
                msend, mrecv, me, sib,
            ).wait_recv()
            valid_total = meta_all[0, 1:2, :]
            for d in range(1, n):
                valid_total = valid_total + meta_all[d, 1:2, :]

            def spell(slot, c):
                target = spread(meta_all[slot, 0:1, :])
                valid = (row_number < meta_all[slot, 1:2, :]).astype(F32) / valid_total
                for t in range(S):
                    place = piece_rows(t, slot)
                    target_col[place, :] = target[t * q:(t + 1) * q]
                    valid_col[place, :] = valid[t * q:(t + 1) * q]
                return c

            lax.fori_loop(0, n, spell, 0)

        share1(s)[1]()
        factor = combine(stat1, s)[2]
        base = s * per_round
        residuals(base, per_round, factor, True)
        swap(r_scr, base, per_round, rsend.at[s], rrecv.at[s], k).start()
        swap(fw_scr, base, per_round, fsend.at[s], frecv.at[s], k).start()

        @pl.when(s == S - 1)
        def _():
            part = jnp.sum(jnp.sum(fsum[...], axis=0, keepdims=True), axis=1, keepdims=True)
            damp_all[mine] = jnp.broadcast_to(part, damp_all.shape[1:])
            start_d()

    def task_gradient(s, c):
        rows = round_rows(s)

        def go(i, carry):
            part = feature_part(i)
            block = xt[part, rows]
            moved[part, columns(c)] += jnp.dot(
                block, r_scr[c, rows, :], preferred_element_type=F32
            )
            inv[c, part, :] += jnp.dot(
                block * block, fw_scr[c, rows, :], preferred_element_type=F32
            )
            return carry

        lax.fori_loop(0, parts, go, 0, unroll=4)

    def when_round(s, act):
        @pl.when(jnp.logical_and(s >= 0, s < S))
        def _():
            act(s)

    def tasks(p, at):
        r = p - late - 1
        if at == TASK_L:
            when_round(r, task_logits)
        if at == TASK_R:
            when_round(r - 1, task_residual)
        if at == TASK_OWN:
            when_round(r - 1, lambda s: task_gradient(s, k))

            @pl.when(p == 0)
            def _():
                lax.fori_loop(0, parts, clear, 0)
        if at == TASK_SIB:
            def other(s):
                base = s * per_round
                swap(r_scr, base, per_round, rsend.at[s], rrecv.at[s], sib).wait_recv()
                swap(fw_scr, base, per_round, fsend.at[s], frecv.at[s], sib).wait_recv()
                task_gradient(s, sib)

            when_round(r - 1, other)

    lax.fori_loop(0, parts, lower, 0)

    def period(p, c):
        for i in range(7):
            if i == OWN_AT:
                when_round(p + ahead, lambda s: own_sends(s, begin))
            if Y == 2:
                event(p, i, True, begin)
            elif i == 0:
                when_round(p, lambda s: line(s, True, begin))
            tasks(p, i)
        return c

    lax.fori_loop(0, S + late + 2, period, 0)

    in_d()
    fisher_sum = damp_all[0, 0:1, 0:1]
    for d in range(1, nd):
        fisher_sum = fisher_sum + damp_all[d, 0:1, 0:1]
    damping = DAMPING_SHARE * fisher_sum / scale + EPSILON

    def update(i, c):
        part = feature_part(i)
        inverse = 1.0 / (inv[c, part, :] + damping)
        inv[c, part, :] = inverse
        change = moved[part, columns(c)] * inverse
        moved[part, columns(c)] = change
        return (w[part, columns(c)] - LEARNING_RATE * change).astype(BF16)

    def low_second(i):
        return remote(
            low_out.at[feature_part(i)], wlow.at[k, feature_part(i)],
            lsend.at[i], lrecv.at[i], me, sib,
        )

    def update_both(i):
        part = feature_part(i)
        low_out[part, :] = update(i, sib)
        low_second(i).start()
        low = update(i, k)
        term = jnp.dot(x[k, :, part], low, preferred_element_type=F32)
        if i == 0:
            e_scr[...] = term
        else:
            e_scr[...] += term

    for i in range(parts):
        update_both(i)

    def low_arrive(i, c):
        part = wlow.at[sib, feature_part(i)]
        remote(part, part, lsend.at[i], lrecv.at[i], me, sib).wait_recv()
        return c

    lax.fori_loop(0, parts, low_arrive, 0)

    def second(b, c):
        rows = pl.ds(pl.multiple_of(b * HALF_ROWS, HALF_ROWS), HALF_ROWS)
        logits = e_scr[rows, :] + jnp.dot(
            x[sib, rows, :], wlow[sib], preferred_element_type=F32
        )
        tile = exponents(b * HALF_ROWS, HALF_ROWS, logits, True)
        stat2[b, mine] = tile[0:2 * per_half, :]
        labels_all[mine, pl.ds(b * per_half, per_half), :] = tile[2 * per_half:3 * per_half, :]
        share2(b)[0]()
        return c

    lax.fori_loop(0, halves, second, 0)

    start_l, in_l, out_l = share(
        labels_all.at[mine], dsend.at[1], drecv.at[1], labels_all.at[pl.ds(0, nd - 1)]
    )
    start_l()

    def rounds_out(s, c):
        swap(r_scr, s * per_round, per_round, rsend.at[s], rrecv.at[s], k).wait_send()
        swap(fw_scr, s * per_round, per_round, fsend.at[s], frecv.at[s], k).wait_send()
        return c

    lax.fori_loop(0, S, rounds_out, 0)

    def drain(p, c):
        when_round(p, lambda s: own_sends(s, finish))
        if Y == 2:
            for i in range(7):
                event(p, i, False, finish)
        else:
            when_round(p, lambda s: line(s, False, finish))

        def rest(s):
            everything = x.at[k, round_rows(s)]
            remote(
                everything, everything, sib_send.at[s], sib_recv.at[s], me, sib
            ).wait_send()
            share1(s)[2]()

        when_round(p, rest)
        return c

    lax.fori_loop(0, S + late, drain, 0)
    remote(
        meta_all.at[pl.ds(0, n - 1)], meta_all.at[pl.ds(0, n - 1)], msend, mrecv, me, sib
    ).wait_send()
    out_d()

    def parts_out(i, c):
        low_second(i).wait_send()
        return c

    lax.fori_loop(0, parts, parts_out, 0)

    def swap2(b, owner):
        return swap(r_scr, b * HALF_ROWS, HALF_ROWS, r2send.at[b], r2recv.at[b], owner)

    def finish_losses():
        in_l()

        for t in range(halves):
            names = slice(t * per_half, (t + 1) * per_half)
            label = labels_all[0, names, :]
            for d in range(1, nd):
                label = label + labels_all[d, names, :]
            loss = loss_row[t] - label
            for j in range(per_half):
                at = t * HALF_ROWS + j * LANES
                loss_col[at:at + LANES, :] = spread(loss[j:j + 1])
        own = jnp.concatenate([loss_col[piece_rows(s, me), :] for s in range(S)], axis=0).T
        losses[...] = (lane_float[0:1] < count).astype(F32) * own[0:1, :]

    def last(b, c):
        rows = pl.ds(pl.multiple_of(b * HALF_ROWS, HALF_ROWS), HALF_ROWS)
        sign = jnp.where(b == 0, -1.0, 1.0).astype(F32)
        share2(b)[1]()
        peak, total, factor = combine(stat2, b)
        residuals(b * HALF_ROWS, HALF_ROWS, factor, False)
        swap2(b, k).start()
        loss_row[b] = peak + jnp.log(total)

        def gradient(owner):
            def go(i, carry):
                part = feature_part(i)
                grad = jnp.dot(xt[part, rows], r_scr[owner, rows, :], preferred_element_type=F32)
                moved[part, columns(owner)] = (
                    sign * moved[part, columns(owner)] - grad * inv[owner, part, :]
                )
                return carry

            lax.fori_loop(0, parts, go, 0, unroll=4)

        gradient(k)
        pl.when(b == halves - 1)(finish_losses)
        swap2(b, sib).wait_recv()
        gradient(sib)
        return c

    lax.fori_loop(0, halves, last, 0)

    out_l()

    def halves_out(b, c):
        share2(b)[2]()
        swap2(b, k).wait_send()
        return c

    lax.fori_loop(0, halves, halves_out, 0)


def solution(mesh):
    n = mesh.shape["example"]
    Y = 2 if n == 8 else 1
    Z = n // Y
    nd = 2 * n

    def body(features, weights, labels, counts, active):
        rows_n, half = features.shape
        local = weights.shape[1]
        ck = local // 2
        all_rows = rows_n * n
        halves = all_rows // HALF_ROWS
        scale = float(half * 2 * local * n)
        parts = half // min(512, half)
        dma = pltpu.SemaphoreType.DMA
        moved, losses = pl.pallas_call(
            functools.partial(kernel, Z, Y, scale),
            out_shape=(
                pltpu.VMEM(weights.shape, F32),
                jax.ShapeDtypeStruct((1, rows_n), F32),
            ),
            in_specs=[
                pl.BlockSpec(memory_space=pl.ANY),
                pl.BlockSpec(memory_space=pl.ANY),
                pl.BlockSpec(memory_space=pltpu.VMEM),
                pl.BlockSpec(memory_space=pltpu.SMEM),
                pl.BlockSpec(memory_space=pltpu.SMEM),
            ],
            out_specs=(
                pl.BlockSpec(memory_space=pltpu.VMEM),
                pl.BlockSpec(memory_space=pltpu.VMEM),
            ),
            scratch_shapes=[
                pltpu.VMEM((2, all_rows, half), BF16),
                pltpu.VMEM((half, all_rows), BF16),
                pltpu.VMEM((half, local), F32),
                pltpu.VMEM((2, half, ck), BF16),
                pltpu.VMEM((half, ck), BF16),
                pltpu.VMEM((all_rows, ck), F32),
                pltpu.VMEM((2, all_rows, ck), BF16),
                pltpu.VMEM((2, all_rows, ck), BF16),
                pltpu.VMEM((2, half, ck), F32),
                pltpu.VMEM((n, 8, rows_n), F32),
                pltpu.VMEM((all_rows, LANES), F32),
                pltpu.VMEM((all_rows, LANES), F32),
                pltpu.VMEM((all_rows, LANES), F32),
                pltpu.VMEM((LANES, LANES), F32),
                pltpu.VMEM((ROUNDS, nd, 2 * (all_rows // ROUNDS // LANES), LANES), F32),
                pltpu.VMEM((halves, nd, 2 * (HALF_ROWS // LANES), LANES), F32),
                pltpu.VMEM((nd, 1, LANES), F32),
                pltpu.VMEM((nd, all_rows // LANES, LANES), F32),
                pltpu.VMEM((halves, HALF_ROWS // LANES, LANES), F32),
                pltpu.VMEM((all_rows, LANES), F32),
                dma((ROUNDS,)), dma((parts,)),
                dma((3, ROUNDS, n)), dma((ROUNDS, n)),
                dma((ROUNDS,)), dma((ROUNDS,)),
                dma((parts,)), dma((parts,)), dma((parts,)), dma((parts,)),
                dma, dma,
                dma((ROUNDS,)), dma((ROUNDS,)), dma((halves,)), dma((halves,)), dma((2,)), dma((2,)),
                dma((ROUNDS,)), dma((ROUNDS,)), dma((ROUNDS,)), dma((ROUNDS,)),
                dma((halves,)), dma((halves,)),
            ],
            compiler_params=pltpu.CompilerParams(
                collective_id=0, has_side_effects=True, vmem_limit_bytes=57671680
            ),
        )(features, weights, labels.reshape(1, rows_n), counts, active)
        return moved, losses.reshape(rows_n)

    return jax.shard_map(
        body,
        mesh=mesh,
        in_specs=(
            P(("groups", "example"), "cls"),
            P(("groups", "cls"), "example"),
            P(("groups", "example")),
            P(("groups", "example")),
            P("groups"),
        ),
        out_specs=(P(("groups", "cls"), "example"), P(("groups", "example"))),
        check_vma=False,
    )
```

```python
import functools

import jax
import jax.numpy as jnp
from jax import lax
from jax.experimental import pallas as pl
from jax.experimental.pallas import tpu as pltpu
from jax.sharding import PartitionSpec as P

NEGATIVE = -1e30
LEARNING_RATE = 2e-05
DAMPING_SHARE = 0.1
EPSILON = 1e-06
MESH = pl.DeviceIdType.MESH
INWARD, OUTWARD, SIDE = 0, 1, 2
F32, BF16 = jnp.float32, jnp.bfloat16

ROUNDS = 4
LANES = 128
HALF_ROWS = 512
AHEAD = 3
OWN_AT = 2
AT_END = "DCEAFBG"
AT_END_LAG = (0, 1, 1, 0, 1, 0, 1)
AT_MID = "ABEGDFC"
AT_MID_LAG = (0, 0, 1, 1, 0, 1, 0)
END_OFFSET = dict(A=1, B=2, C=3, D=0, E=1, F=2, G=3)
MID_OFFSET = dict(A=-1, B=1, C=2, D=0, E=1, F=-1, G=2)
TASK_L, TASK_R, TASK_OWN, TASK_SIB = 0, 4, 5, 6


def kernel(
    Z, Y, scale,
    features, weights, labels, counts, active,
    moved, losses,
    x, xt, w, wlow, low_out, e_scr, r_scr, fw_scr, inv,
    meta_all, target_col, valid_col, ssq, fsum, stat1, stat2, damp_all, labels_all, loss_row, loss_col,
    own_sem, w_sem, gsend, grecv, sib_send, sib_recv,
    wsend, wrecv, lsend, lrecv, msend, mrecv,
    s1send, s1recv, s2send, s2recv, dsend, drecv,
    rsend, rrecv, fsend, frecv, r2send, r2recv,
):
    n = Z * Y
    nd = 2 * n
    rows_n, half = features.shape
    S = ROUNDS
    q = rows_n // S
    per_round = n * q
    groups = per_round // LANES
    all_rows = n * rows_n
    ck = moved.shape[1] // 2
    step = min(512, half)
    parts = half // step
    halves = all_rows // HALF_ROWS
    per_half = HALF_ROWS // LANES
    me = lax.axis_index("example")
    k = lax.axis_index("cls")
    sib = 1 - k
    z, y = me // Y, lax.rem(me, Y)
    mine = me * 2 + k
    inward = jnp.where(z < Z // 2, 1, -1)
    is_end = jnp.logical_or(z == 0, z == Z - 1)
    is_mid = jnp.logical_not(is_end)

    def round_rows(s):
        return pl.ds(pl.multiple_of(s * per_round, per_round), per_round)

    def piece_rows(s, slot):
        return pl.ds(pl.multiple_of(s * per_round + slot * q, q), q)

    def columns(c):
        return pl.ds(pl.multiple_of(c * ck, ck), ck)

    def feature_part(i):
        return pl.ds(pl.multiple_of(i * step, step), step)

    def remote(src, dst, ssem, rsem, example, core):
        return pltpu.make_async_remote_copy(
            src_ref=src, dst_ref=dst, send_sem=ssem, recv_sem=rsem,
            device_id={"example": example, "cls": core}, device_id_type=MESH,
        )

    def own_piece(s):
        return features.at[pl.ds(pl.multiple_of(s * q, q), q)]

    def own_copy(s):
        return pltpu.make_async_copy(own_piece(s), x.at[k, piece_rows(s, me)], own_sem.at[s])

    def w_copy(i):
        return pltpu.make_async_copy(
            weights.at[feature_part(i)], w.at[feature_part(i)], w_sem.at[i]
        )

    for s in range(S):
        own_copy(s).start()
    for i in range(parts):
        w_copy(i).start()

    barrier = pltpu.get_barrier_semaphore()

    def greet(example, core):
        pl.semaphore_signal(
            barrier, inc=1, device_id={"example": example, "cls": core}, device_id_type=MESH
        )

    greet(me, sib)
    if Y == 2:
        greet(z * Y + (1 - y), k)

    @pl.when(z < Z - 1)
    def _():
        greet(me + Y, k)

    @pl.when(z > 0)
    def _():
        greet(me - Y, k)

    pl.semaphore_wait(barrier, Y + (z < Z - 1).astype(jnp.int32) + (z > 0).astype(jnp.int32))

    def forward(direction, s, slot, src):
        target = {
            INWARD: me + inward * Y,
            OUTWARD: me - inward * Y,
            SIDE: z * Y + (Y - 1 - y),
        }[direction]
        return remote(
            src, x.at[k, piece_rows(s, slot)], gsend.at[direction, s, slot],
            grecv.at[s, slot], target, k,
        )

    def to_sibling(s, slot, src):
        return remote(
            src, x.at[k, piece_rows(s, slot)], sib_send.at[s], sib_recv.at[s], me, sib
        )

    def arrived(s, slot):
        place = x.at[k, piece_rows(s, slot)]
        remote(place, place, gsend.at[SIDE, s, slot], grecv.at[s, slot], me, sib).wait_recv()

    def has_outer():
        return jnp.logical_and(z - inward >= 0, z - inward < Z)

    def own_sends(s, act):
        src = own_piece(s)
        act(forward(INWARD, s, me, src))

        @pl.when(has_outer())
        def _():
            act(forward(OUTWARD, s, me, src))

        if Y == 2:
            act(forward(SIDE, s, me, src))

    def begin(copy):
        copy.start()

    def finish(copy):
        copy.wait_send()

    def event(p, i, receive, act):
        end, mid = AT_END[i], AT_MID[i]
        s = p - jnp.where(is_end, AT_END_LAG[i], AT_MID_LAG[i])
        zz = z + inward * jnp.where(is_end, END_OFFSET[end], MID_OFFSET[mid])
        across = jnp.where(is_end, int(end in "DEFG"), int(mid in "DEFG"))
        slot = zz * Y + jnp.where(across == 1, 1 - y, y)
        odd = lax.rem(s, 2) == 1

        def any_of(*terms):
            out = None
            for use, condition in terms:
                if use:
                    out = condition if out is None else jnp.logical_or(out, condition)
            return out

        side = any_of(
            (end in "AB", is_end),
            (end == "C", jnp.logical_and(is_end, jnp.logical_not(odd))),
            (mid in "BC", is_mid),
        )
        inner = any_of((end == "D", is_end), (mid == "A", is_mid))
        outer = any_of((mid in "BC", is_mid), (mid == "G", jnp.logical_and(is_mid, odd)))

        @pl.when(jnp.logical_and(s >= 0, s < S))
        def _():
            src = x.at[k, piece_rows(s, slot)]
            if receive:
                arrived(s, slot)
            for condition, direction in ((outer, OUTWARD), (side, SIDE), (inner, INWARD)):
                if condition is not None:
                    @pl.when(condition)
                    def _():
                        act(forward(direction, s, slot, src))
            if receive:
                to_sibling(s, slot, src).start()

    def line(s, receive, act):
        def go(j, c):
            for sign in (-1, 1):
                zz = z + sign * j

                @pl.when(jnp.logical_and(zz >= 0, zz < Z))
                def _():
                    src = x.at[k, piece_rows(s, zz)]
                    if receive:
                        arrived(s, zz)
                    toward = jnp.where(inward == -sign, INWARD, OUTWARD)
                    target = z - sign

                    @pl.when(jnp.logical_and(target >= 0, target < Z))
                    def _():
                        act(remote(
                            src, src, gsend.at[toward, s, zz], grecv.at[s, zz], target, k
                        ))
                    if receive:
                        to_sibling(s, zz, src).start()
            return c

        lax.fori_loop(1, Z, go, 0)

    if Y == 2:
        assert Z == 4
        late = max(AT_END_LAG + AT_MID_LAG)
    else:
        late = 0
    ahead = min(AHEAD, S)

    for s in range(ahead):
        own_sends(s, begin)
    for s in range(S):
        to_sibling(s, me, own_piece(s)).start()

    def low_first(i):
        return remote(
            low_out.at[feature_part(i)], wlow.at[k, feature_part(i)],
            wsend.at[i], wrecv.at[i], me, sib,
        )

    def lower(i, c):
        part = feature_part(i)
        w_copy(i).wait()
        low_out[part, :] = w[part, columns(sib)].astype(BF16)
        low_first(i).start()
        wlow[k, part, :] = w[part, columns(k)].astype(BF16)
        return c

    def meta_copy(p):
        peer = lax.rem(me + p, n)
        return remote(meta_all.at[me], meta_all.at[me], msend, mrecv, peer, k)

    count = counts[0].astype(F32)
    label = labels[...]
    target_row = jnp.where(label >= active[0], label - active[0], label).astype(F32)
    meta_row = lax.broadcasted_iota(jnp.int32, (8, rows_n), 0)
    meta_all[me] = jnp.where(meta_row == 0, jnp.broadcast_to(target_row, (8, rows_n)), count)
    fsum[...] = jnp.zeros_like(fsum)

    active_count = active[0]
    class_base = mine * ck
    lane = lax.broadcasted_iota(jnp.int32, (LANES, LANES), 1)
    lane_float = lane.astype(F32)
    row_number = lax.broadcasted_iota(jnp.int32, (LANES, LANES), 0).astype(F32)

    def spread(row):
        return jnp.broadcast_to(row, (LANES, LANES)).T

    def share(piece, ssem, rsem, everyone):
        def copy(p):
            peer = lax.rem(mine + p, nd)
            return remote(piece, piece, ssem, rsem, peer // 2, lax.rem(peer, 2))

        def start():
            def go(i, c):
                copy(nd // 2 + (1 - 2 * lax.rem(i, 2)) * ((i + 1) // 2)).start()
                return c

            lax.fori_loop(0, nd - 1, go, 0)

        def wait_in():
            remote(everyone, everyone, ssem, rsem, me, sib).wait_recv()

        def wait_out():
            remote(everyone, everyone, ssem, rsem, me, sib).wait_send()

        return start, wait_in, wait_out

    def share1(s):
        return share(
            stat1.at[s, mine], s1send.at[s], s1recv.at[s], stat1.at[s, pl.ds(0, nd - 1)]
        )

    def share2(b):
        return share(
            stat2.at[b, mine], s2send.at[b], s2recv.at[b], stat2.at[b, pl.ds(0, nd - 1)]
        )

    def exponents(base, rows, logits, with_label):
        index = class_base + lax.broadcasted_iota(jnp.int32, (rows, ck), 1)
        masked = jnp.where(index < active_count, logits, NEGATIVE)
        peak = jnp.max(masked, axis=1, keepdims=True)
        exponent = jnp.exp(masked - peak)
        total = jnp.sum(exponent, axis=1, keepdims=True)
        place = slice(base, base + rows) if isinstance(base, int) else pl.ds(pl.multiple_of(base, rows), rows)
        e_scr[place, :] = exponent
        if with_label:
            target = target_col[place, 0:1]
            label = jnp.sum(
                jnp.where(index.astype(F32) == target, logits, 0.0), axis=1, keepdims=True
            )
        count_rows = rows // LANES
        tile = jnp.zeros((LANES, LANES), F32)
        for j in range(count_rows):
            part = slice(j * LANES, (j + 1) * LANES)
            tile = jnp.where(lane == j, peak[part], tile)
            tile = jnp.where(lane == count_rows + j, total[part], tile)
            if with_label:
                tile = jnp.where(lane == 2 * count_rows + j, label[part], tile)
        return tile.T

    def combine(stat, b):
        count_rows = stat.shape[2] // 2
        tops, sums = slice(0, count_rows), slice(count_rows, 2 * count_rows)
        peak = stat[b, 0, tops]
        for d in range(1, nd):
            peak = jnp.maximum(peak, stat[b, d, tops])
        total = jnp.zeros_like(peak)
        for d in range(nd):
            total = total + stat[b, d, sums] * jnp.exp(stat[b, d, tops] - peak)
        return peak, total, jnp.exp(stat[b, mine, tops] - peak) / total

    def residuals(base, rows, factor, first):
        for j in range(rows // LANES):
            place = pl.ds(pl.multiple_of(base + j * LANES, LANES), LANES)
            weight = spread(factor[j:j + 1])
            valid = valid_col[place, :]
            target = target_col[place, :]
            if first:
                square = ssq[place, :]
            for c in range(ck // LANES):
                cols = slice(c * LANES, (c + 1) * LANES)
                probability = e_scr[place, cols] * weight
                index = lane_float + (class_base + c * LANES).astype(F32)
                is_label = (index == target).astype(F32)
                r_scr[k, place, cols] = (valid * (probability - is_label)).astype(BF16)
                if first:
                    fw = (valid * probability * (1.0 - probability)).astype(BF16)
                    fw_scr[k, place, cols] = fw
                    fsum[...] += fw.astype(F32) * square

    def swap(buffer, base, rows, ssem, rsem, owner):
        place = buffer.at[owner, pl.ds(pl.multiple_of(base, rows), rows)]
        return remote(place, place, ssem, rsem, me, sib)

    def clear(i, c):
        part = feature_part(i)
        moved[part, :] = jnp.zeros((step, 2 * ck), F32)
        for h in range(2):
            inv[h, part, :] = jnp.zeros((step, ck), F32)
        return c

    def task_logits(s):
        rows = round_rows(s)
        everything = x.at[sib, rows]
        own_copy(s).wait()
        remote(everything, everything, sib_send.at[s], sib_recv.at[s], me, sib).wait_recv()

        @pl.when(s == 0)
        def _():
            def arrive(i, c):
                part = wlow.at[sib, feature_part(i)]
                remote(part, part, wsend.at[i], wrecv.at[i], me, sib).wait_recv()
                low_first(i).wait_send()
                return c

            lax.fori_loop(0, parts, arrive, 0)

            def meta_start(p, c):
                meta_copy(p).start()
                return c

            lax.fori_loop(1, n, meta_start, 0)

        logits = jnp.dot(x[0, rows, :], wlow[0], preferred_element_type=F32)
        logits = logits + jnp.dot(x[1, rows, :], wlow[1], preferred_element_type=F32)
        tile = exponents(s * per_round, per_round, logits, False)
        stat1[s, mine] = tile[0:2 * groups, :]
        share1(s)[0]()
        squares = jnp.zeros((per_round, 1), F32)
        for h in range(2):
            block = x[h, rows, :]
            squares = squares + jnp.sum((block * block).astype(F32), axis=1, keepdims=True)
        ssq[rows, :] = jnp.broadcast_to(squares, (per_round, LANES))
        xt[:, rows] = x[k, rows, :].T

    start_d, in_d, out_d = share(
        damp_all.at[mine], dsend.at[0], drecv.at[0], damp_all.at[pl.ds(0, nd - 1)]
    )

    def task_residual(s):
        @pl.when(s == 0)
        def _():
            remote(
                meta_all.at[pl.ds(0, n - 1)], meta_all.at[pl.ds(0, n - 1)],
                msend, mrecv, me, sib,
            ).wait_recv()
            valid_total = meta_all[0, 1:2, :]
            for d in range(1, n):
                valid_total = valid_total + meta_all[d, 1:2, :]

            def spell(slot, c):
                target = spread(meta_all[slot, 0:1, :])
                valid = (row_number < meta_all[slot, 1:2, :]).astype(F32) / valid_total
                for t in range(S):
                    place = piece_rows(t, slot)
                    target_col[place, :] = target[t * q:(t + 1) * q]
                    valid_col[place, :] = valid[t * q:(t + 1) * q]
                return c

            lax.fori_loop(0, n, spell, 0)

        share1(s)[1]()
        factor = combine(stat1, s)[2]
        base = s * per_round
        residuals(base, per_round, factor, True)
        swap(r_scr, base, per_round, rsend.at[s], rrecv.at[s], k).start()
        swap(fw_scr, base, per_round, fsend.at[s], frecv.at[s], k).start()

        @pl.when(s == S - 1)
        def _():
            part = jnp.sum(jnp.sum(fsum[...], axis=0, keepdims=True), axis=1, keepdims=True)
            damp_all[mine] = jnp.broadcast_to(part, damp_all.shape[1:])
            start_d()

    def task_gradient(s, c):
        rows = round_rows(s)

        def go(i, carry):
            part = feature_part(i)
            block = xt[part, rows]
            moved[part, columns(c)] += jnp.dot(
                block, r_scr[c, rows, :], preferred_element_type=F32
            )
            inv[c, part, :] += jnp.dot(
                block * block, fw_scr[c, rows, :], preferred_element_type=F32
            )
            return carry

        lax.fori_loop(0, parts, go, 0, unroll=4)

    def when_round(s, act):
        @pl.when(jnp.logical_and(s >= 0, s < S))
        def _():
            act(s)

    def tasks(p, at):
        r = p - late - 1
        if at == TASK_L:
            when_round(r, task_logits)
        if at == TASK_R:
            when_round(r - 1, task_residual)
        if at == TASK_OWN:
            when_round(r - 1, lambda s: task_gradient(s, k))

            @pl.when(p == 0)
            def _():
                lax.fori_loop(0, parts, clear, 0)
        if at == TASK_SIB:
            def other(s):
                base = s * per_round
                swap(r_scr, base, per_round, rsend.at[s], rrecv.at[s], sib).wait_recv()
                swap(fw_scr, base, per_round, fsend.at[s], frecv.at[s], sib).wait_recv()
                task_gradient(s, sib)

            when_round(r - 1, other)

    lax.fori_loop(0, parts, lower, 0)

    def period(p, c):
        for i in range(7):
            if i == OWN_AT:
                when_round(p + ahead, lambda s: own_sends(s, begin))
            if Y == 2:
                event(p, i, True, begin)
            elif i == 0:
                when_round(p, lambda s: line(s, True, begin))
            tasks(p, i)
        return c

    lax.fori_loop(0, S + late + 2, period, 0)

    in_d()
    fisher_sum = damp_all[0, 0:1, 0:1]
    for d in range(1, nd):
        fisher_sum = fisher_sum + damp_all[d, 0:1, 0:1]
    damping = DAMPING_SHARE * fisher_sum / scale + EPSILON

    def update(i, c):
        part = feature_part(i)
        inverse = 1.0 / (inv[c, part, :] + damping)
        inv[c, part, :] = inverse
        change = moved[part, columns(c)] * inverse
        moved[part, columns(c)] = change
        return (w[part, columns(c)] - LEARNING_RATE * change).astype(BF16)

    def low_second(i):
        return remote(
            low_out.at[feature_part(i)], wlow.at[k, feature_part(i)],
            lsend.at[i], lrecv.at[i], me, sib,
        )

    def update_both(i):
        part = feature_part(i)
        low_out[part, :] = update(i, sib)
        low_second(i).start()
        low = update(i, k)
        term = jnp.dot(x[k, :, part], low, preferred_element_type=F32)
        if i == 0:
            e_scr[...] = term
        else:
            e_scr[...] += term

    for i in range(parts):
        update_both(i)

    def low_arrive(i, c):
        part = wlow.at[sib, feature_part(i)]
        remote(part, part, lsend.at[i], lrecv.at[i], me, sib).wait_recv()
        return c

    lax.fori_loop(0, parts, low_arrive, 0)

    def second(b, c):
        rows = pl.ds(pl.multiple_of(b * HALF_ROWS, HALF_ROWS), HALF_ROWS)
        logits = e_scr[rows, :] + jnp.dot(
            x[sib, rows, :], wlow[sib], preferred_element_type=F32
        )
        tile = exponents(b * HALF_ROWS, HALF_ROWS, logits, True)
        stat2[b, mine] = tile[0:2 * per_half, :]
        labels_all[mine, pl.ds(b * per_half, per_half), :] = tile[2 * per_half:3 * per_half, :]
        share2(b)[0]()
        return c

    lax.fori_loop(0, halves, second, 0)

    start_l, in_l, out_l = share(
        labels_all.at[mine], dsend.at[1], drecv.at[1], labels_all.at[pl.ds(0, nd - 1)]
    )
    start_l()

    def rounds_out(s, c):
        swap(r_scr, s * per_round, per_round, rsend.at[s], rrecv.at[s], k).wait_send()
        swap(fw_scr, s * per_round, per_round, fsend.at[s], frecv.at[s], k).wait_send()
        return c

    lax.fori_loop(0, S, rounds_out, 0)

    def drain(p, c):
        when_round(p, lambda s: own_sends(s, finish))
        if Y == 2:
            for i in range(7):
                event(p, i, False, finish)
        else:
            when_round(p, lambda s: line(s, False, finish))

        def rest(s):
            everything = x.at[k, round_rows(s)]
            remote(
                everything, everything, sib_send.at[s], sib_recv.at[s], me, sib
            ).wait_send()
            share1(s)[2]()

        when_round(p, rest)
        return c

    lax.fori_loop(0, S + late, drain, 0)
    remote(
        meta_all.at[pl.ds(0, n - 1)], meta_all.at[pl.ds(0, n - 1)], msend, mrecv, me, sib
    ).wait_send()
    out_d()

    def parts_out(i, c):
        low_second(i).wait_send()
        return c

    lax.fori_loop(0, parts, parts_out, 0)

    def swap2(b, owner):
        return swap(r_scr, b * HALF_ROWS, HALF_ROWS, r2send.at[b], r2recv.at[b], owner)

    def finish_losses():
        in_l()

        for t in range(halves):
            names = slice(t * per_half, (t + 1) * per_half)
            label = labels_all[0, names, :]
            for d in range(1, nd):
                label = label + labels_all[d, names, :]
            loss = loss_row[t] - label
            for j in range(per_half):
                at = t * HALF_ROWS + j * LANES
                loss_col[at:at + LANES, :] = spread(loss[j:j + 1])
        own = jnp.concatenate([loss_col[piece_rows(s, me), :] for s in range(S)], axis=0).T
        losses[...] = (lane_float[0:1] < count).astype(F32) * own[0:1, :]

    def last(b, c):
        rows = pl.ds(pl.multiple_of(b * HALF_ROWS, HALF_ROWS), HALF_ROWS)
        sign = jnp.where(b == 0, -1.0, 1.0).astype(F32)
        share2(b)[1]()
        peak, total, factor = combine(stat2, b)
        residuals(b * HALF_ROWS, HALF_ROWS, factor, False)
        swap2(b, k).start()
        loss_row[b] = peak + jnp.log(total)

        def gradient(owner):
            def go(i, carry):
                part = feature_part(i)
                grad = jnp.dot(xt[part, rows], r_scr[owner, rows, :], preferred_element_type=F32)
                moved[part, columns(owner)] = (
                    sign * moved[part, columns(owner)] - grad * inv[owner, part, :]
                )
                return carry

            lax.fori_loop(0, parts, go, 0, unroll=4)

        gradient(k)
        pl.when(b == halves - 1)(finish_losses)
        swap2(b, sib).wait_recv()
        gradient(sib)
        return c

    lax.fori_loop(0, halves, last, 0)

    out_l()

    def halves_out(b, c):
        share2(b)[2]()
        swap2(b, k).wait_send()
        return c

    lax.fori_loop(0, halves, halves_out, 0)


def solution(mesh):
    n = mesh.shape["example"]
    Y = 2 if n == 8 else 1
    Z = n // Y
    nd = 2 * n

    def body(features, weights, labels, counts, active):
        rows_n, half = features.shape
        local = weights.shape[1]
        ck = local // 2
        all_rows = rows_n * n
        halves = all_rows // HALF_ROWS
        scale = float(half * 2 * local * n)
        parts = half // min(512, half)
        dma = pltpu.SemaphoreType.DMA
        moved, losses = pl.pallas_call(
            functools.partial(kernel, Z, Y, scale),
            out_shape=(
                pltpu.VMEM(weights.shape, F32),
                jax.ShapeDtypeStruct((1, rows_n), F32),
            ),
            in_specs=[
                pl.BlockSpec(memory_space=pl.ANY),
                pl.BlockSpec(memory_space=pl.ANY),
                pl.BlockSpec(memory_space=pltpu.VMEM),
                pl.BlockSpec(memory_space=pltpu.SMEM),
                pl.BlockSpec(memory_space=pltpu.SMEM),
            ],
            out_specs=(
                pl.BlockSpec(memory_space=pltpu.VMEM),
                pl.BlockSpec(memory_space=pltpu.VMEM),
            ),
            scratch_shapes=[
                pltpu.VMEM((2, all_rows, half), BF16),
                pltpu.VMEM((half, all_rows), BF16),
                pltpu.VMEM((half, local), F32),
                pltpu.VMEM((2, half, ck), BF16),
                pltpu.VMEM((half, ck), BF16),
                pltpu.VMEM((all_rows, ck), F32),
                pltpu.VMEM((2, all_rows, ck), BF16),
                pltpu.VMEM((2, all_rows, ck), BF16),
                pltpu.VMEM((2, half, ck), F32),
                pltpu.VMEM((n, 8, rows_n), F32),
                pltpu.VMEM((all_rows, LANES), F32),
                pltpu.VMEM((all_rows, LANES), F32),
                pltpu.VMEM((all_rows, LANES), F32),
                pltpu.VMEM((LANES, LANES), F32),
                pltpu.VMEM((ROUNDS, nd, 2 * (all_rows // ROUNDS // LANES), LANES), F32),
                pltpu.VMEM((halves, nd, 2 * (HALF_ROWS // LANES), LANES), F32),
                pltpu.VMEM((nd, 1, LANES), F32),
                pltpu.VMEM((nd, all_rows // LANES, LANES), F32),
                pltpu.VMEM((halves, HALF_ROWS // LANES, LANES), F32),
                pltpu.VMEM((all_rows, LANES), F32),
                dma((ROUNDS,)), dma((parts,)),
                dma((3, ROUNDS, n)), dma((ROUNDS, n)),
                dma((ROUNDS,)), dma((ROUNDS,)),
                dma((parts,)), dma((parts,)), dma((parts,)), dma((parts,)),
                dma, dma,
                dma((ROUNDS,)), dma((ROUNDS,)), dma((halves,)), dma((halves,)), dma((2,)), dma((2,)),
                dma((ROUNDS,)), dma((ROUNDS,)), dma((ROUNDS,)), dma((ROUNDS,)),
                dma((halves,)), dma((halves,)),
            ],
            compiler_params=pltpu.CompilerParams(
                collective_id=0, has_side_effects=True, vmem_limit_bytes=57671680
            ),
        )(features, weights, labels.reshape(1, rows_n), counts, active)
        return moved, losses.reshape(rows_n)

    return jax.shard_map(
        body,
        mesh=mesh,
        in_specs=(
            P(("groups", "example"), "cls"),
            P(("groups", "cls"), "example"),
            P(("groups", "example")),
            P(("groups", "example")),
            P("groups"),
        ),
        out_specs=(P(("groups", "cls"), "example"), P(("groups", "example"))),
        check_vma=False,
    )
```
